512 devices in a mesh: facet: 128 (over z, y, core), chan: 4 (over x).
Axes of the slice: x: 4, y: 4, z: 16, core: 2. Of those that a mesh axis runs over, the one named last changes fastest.
Arguments:
- taylor: float32 [128, 4, 4, 8192], P('facet', 'chan'), may hold values from -6 to 6
- chan_coord: float32 [4], replicated, may hold values from -1 to 1
- sub_offset: int32 [64, 2], replicated, may hold values from 0 to 65535
- sub_owner: int32 [64], replicated, may hold values from 0 to 127, as said below
- tile_list: int32 [2048], P('facet'), may hold values from -1 to 127, as said below
- fourier: float32 [2048, 4, 64, 256], P('facet', 'chan'), may hold values from -0.5 to 0.5
Outputs:
- visibilities: float32 [2048, 4, 256], P('facet', 'chan')
The draws below stay inside these ranges and needn't reach their ends.
Inputs may be any that keep to these rules, and one draw needn't show every extreme that they name: `sub_owner`: every position along `facet` owns at most 2 of the listed subgrids, at least one owns exactly 2, and some own none. `tile_list`: on position i along `facet` every entry is -1 where i owns no subgrid, else lies in 0 .. 64 times the number of subgrids i owns, minus one.
All inputs are finite; a program needn't handle non-finite values.
Results may differ from the reference program's by a relative error of at most 0.0003.
Values sent between devices are 32-bit elements; how exact they have to be, the bound alone decides.
A program may use at most 64 MiB of HBM per device.

```python
import math
import jax
import jax.numpy as jnp
from jax import lax

FACET = 8192
SIDE = 8
SKY = 65536
WIN = 64
VIS = 128
TAYLOR = 4
ROWS = 4
NBLK = 16
CAP = 2
BANDS = 128
CHANS = 4
SUBS = 64
N_FACET = 128
N_CHAN = 4


def owner_table(key):
    base_key = jax.random.fold_in(key, 7)
    key_full, key_bits, key_perm = jax.random.split(base_key, 3)
    slot_total = N_FACET * CAP
    full_owner = jax.random.randint(key_full, (), 0, N_FACET)
    slot_ids = jnp.arange(slot_total, dtype=jnp.int32)
    holders = slot_ids // CAP
    random_bits = jax.random.randint(key_bits, (slot_total,), 1, 2 ** 20)
    scores = jnp.where(holders == full_owner, 0, random_bits) * slot_total + slot_ids
    chosen = jnp.argsort(scores)[:SUBS]
    owners = (chosen // CAP).astype(jnp.int32)
    owners = jax.random.permutation(key_perm, owners)
    counts = jnp.sum((owners[None, :] == jnp.arange(N_FACET, dtype=jnp.int32)[:, None]).astype(jnp.int32), axis=1)
    return (owners, counts)


def draw_sub_owner(key, part):
    owners, counts = owner_table(key)
    return owners.astype(jnp.int32)


def draw_tile_list(key, part):
    owners, counts = owner_table(key)
    tile_key = jax.random.fold_in(key, 19)
    random_rows = jax.random.randint(tile_key, (N_FACET, NBLK), 0, 2 ** 20)
    limits = counts * WIN
    bounded = jnp.maximum(limits, 1)
    tiles = random_rows % bounded[:, None]
    tiles = tiles.at[:, 0].set(bounded - 1)
    tiles = tiles.at[:, 1].set(0)
    tiles = jnp.where(limits[:, None] > 0, tiles, -1)
    return tiles.reshape(N_FACET * NBLK).astype(jnp.int32)


def with_ends(drawn, own_key, least, top_value):
    longest = drawn.shape.index(max(drawn.shape))
    spots = []
    for shift in (0, 1):
        where = [jax.random.randint(jax.random.fold_in(own_key, axis), (), 0, length) for axis, length in enumerate(drawn.shape)]
        where[longest] = (where[longest] + shift) % drawn.shape[longest]
        spots.append(tuple(where))
    return drawn.at[spots[0]].set(least).at[spots[1]].set(top_value)


def shard_levels(key, extent, shards, low, largest):
    loudness, own = 1.0, jax.random.fold_in(key, 6)
    for dim, shards_of in shards:
        heights = jnp.exp(jax.random.uniform(jax.random.fold_in(own, dim), (shards_of,), jnp.float32, low / len(shards), largest / len(shards)))
        loudness = loudness * jnp.repeat(heights, extent[dim] // shards_of).reshape([-1 if axis == dim else 1 for axis in range(len(extent))])
    return loudness


def noise(stream_key, extent, width, limit, shards=(), held_as=jnp.bfloat16):
    factor_of = shard_levels(stream_key, extent, shards, -0.22, 0.18) if shards else 1.0
    drawn = jax.random.normal(stream_key, extent, jnp.float32) * width * factor_of
    return jnp.minimum(jnp.maximum(drawn, -limit), limit).astype(held_as)


def setup_inputs(seed: int = 0) -> dict:
    key_list = jax.random.split(jax.random.key(seed), 7)
    taylor = noise(key_list[0], (BANDS, TAYLOR, ROWS, FACET), 1.0, 6.0, ((0, 128), (1, 4)), jnp.float32)
    chan_coord = jnp.clip(jax.random.uniform(key_list[1], (CHANS,), jnp.float32, -1.0, 1.0), -1.0, 1.0)
    sub_offset = with_ends(jax.random.randint(key_list[2], (SUBS, 2), 0, SKY), jax.random.fold_in(key_list[2], 1), 0, SKY - 1).astype(jnp.int32)
    sub_owner = draw_sub_owner(jax.random.fold_in(key_list[6], 71), 0)
    tile_list = draw_tile_list(jax.random.fold_in(key_list[6], 71), 0)
    fourier = noise(key_list[5], (N_FACET * NBLK, CHANS, WIN, 2 * VIS), (2 * WIN) ** -0.5, 0.5, ((0, 128), (1, 4)), jnp.float32)
    return dict(taylor=taylor, chan_coord=chan_coord, sub_offset=sub_offset, sub_owner=sub_owner, tile_list=tile_list, fourier=fourier)


precise = lax.Precision.HIGHEST


def phase_index(left_side, right_side, period):
    low_part = left_side % 256
    high_part = left_side // 256
    wrapped = (low_part * right_side + ((high_part * right_side) % 256) * 256) % 65536
    return wrapped % period


def turn_angle(index_values, period):
    return (2.0 * math.pi / period) * index_values.astype(jnp.float32)


def taylor_powers(chan_coord, order_count):
    columns = [jnp.ones_like(chan_coord)]
    for degree in range(1, order_count):
        columns.append(columns[-1] * chan_coord)
    return jnp.stack(columns, axis=1)


def inverse_window(window, length):
    indices = jnp.arange(length, dtype=jnp.int32)
    angles = turn_angle((indices[:, None] * indices[None, :]) % length, length)
    cosines = jnp.cos(angles)
    sines = jnp.sin(angles)
    real_in = window[..., :length]
    imag_in = window[..., length:]
    real_mid = jnp.einsum("...vu,uw->...vw", real_in, cosines, precision=precise) - jnp.einsum("...vu,uw->...vw", imag_in, sines, precision=precise)
    imag_mid = jnp.einsum("...vu,uw->...vw", real_in, sines, precision=precise) + jnp.einsum("...vu,uw->...vw", imag_in, cosines, precision=precise)
    real_out = jnp.einsum("...vw,vy->...yw", real_mid, cosines, precision=precise) - jnp.einsum("...vw,vy->...yw", imag_mid, sines, precision=precise)
    imag_out = jnp.einsum("...vw,vy->...yw", real_mid, sines, precision=precise) + jnp.einsum("...vw,vy->...yw", imag_mid, cosines, precision=precise)
    return jnp.concatenate([real_out, imag_out], axis=-1) / length


def slot_ranks(sub_owner):
    positions = jnp.arange(sub_owner.shape[0], dtype=jnp.int32)
    earlier = positions[None, :] < positions[:, None]
    same_owner = sub_owner[None, :] == sub_owner[:, None]
    return jnp.sum((earlier & same_owner).astype(jnp.int32), axis=1)


def reference(taylor, chan_coord, sub_offset, sub_owner, tile_list, fourier):
    powers = taylor_powers(chan_coord, TAYLOR)
    channel = jnp.einsum("ct,ftrx->fcrx", powers, taylor, precision=precise)
    band_ids = jnp.arange(N_FACET, dtype=jnp.int32)
    facet_ids = band_ids % (SIDE * SIDE)
    anchor_x = (facet_ids % SIDE) * FACET
    anchor_y = (facet_ids // SIDE) * FACET + (band_ids // (SIDE * SIDE)) * ROWS
    flat_rows = channel.reshape(N_FACET * N_CHAN * ROWS, FACET)
    pixels = jnp.arange(FACET, dtype=jnp.int32)
    freq_steps = jnp.arange(WIN, dtype=jnp.int32)
    row_steps = jnp.arange(ROWS, dtype=jnp.int32)
    factor = float((FACET * ROWS * N_FACET) ** -0.5)

    def one_subgrid(offsets):
        column_freq = (offsets[0] + freq_steps) % SKY
        angles = turn_angle(phase_index(pixels[:, None], column_freq[None, :], SKY), SKY)
        lookup = jnp.concatenate([jnp.cos(angles), -jnp.sin(angles)], axis=1)
        partial_value = jnp.dot(flat_rows, lookup, precision=precise).reshape(N_FACET, N_CHAN, ROWS, 2 * WIN)
        shift_angle = turn_angle(phase_index(anchor_x[:, None], column_freq[None, :], SKY), SKY)[:, None, None, :]
        real_part = partial_value[..., :WIN]
        imag_part = partial_value[..., WIN:]
        real_x = real_part * jnp.cos(shift_angle) + imag_part * jnp.sin(shift_angle)
        imag_x = imag_part * jnp.cos(shift_angle) - real_part * jnp.sin(shift_angle)
        row_freq = (offsets[1] + freq_steps) % SKY
        row_pos = anchor_y[:, None] + row_steps[None, :]
        vertical = turn_angle(phase_index(row_pos[:, None, :], row_freq[None, :, None], SKY), SKY)
        cos_v = jnp.cos(vertical)
        sin_v = jnp.sin(vertical)
        real_w = jnp.einsum("nvr,ncru->cvu", cos_v, real_x, precision=precise) + jnp.einsum("nvr,ncru->cvu", sin_v, imag_x, precision=precise)
        imag_w = jnp.einsum("nvr,ncru->cvu", cos_v, imag_x, precision=precise) - jnp.einsum("nvr,ncru->cvu", sin_v, real_x, precision=precise)
        return jnp.concatenate([real_w, imag_w], axis=-1) * factor

    windows = lax.map(one_subgrid, sub_offset)
    pictures = inverse_window(windows, WIN)
    ranks = slot_ranks(sub_owner)
    tile_ids = tile_list.reshape(N_FACET, NBLK)
    usable = tile_ids >= 0
    clipped = jnp.maximum(tile_ids, 0)
    slot_index = clipped // WIN
    row_index = clipped % WIN
    sub_ids = jnp.arange(SUBS, dtype=jnp.int32)
    matches = (sub_owner[None, None, :] == band_ids[:, None, None]) & (ranks[None, None, :] == slot_index[:, :, None])
    chosen = jnp.sum(jnp.where(matches, sub_ids[None, None, :], 0), axis=2).astype(jnp.int32)
    picked = pictures[chosen, :, row_index, :]
    picked = jnp.where(usable[:, :, None, None], picked, 0.0)
    blocks = fourier.reshape(N_FACET, NBLK, N_CHAN, WIN, 2 * VIS)
    real_t = picked[..., :WIN]
    imag_t = picked[..., WIN:]
    real_f = blocks[..., :VIS]
    imag_f = blocks[..., VIS:]
    real_v = jnp.einsum("nbcy,nbcyz->nbcz", real_t, real_f, precision=precise) - jnp.einsum("nbcy,nbcyz->nbcz", imag_t, imag_f, precision=precise)
    imag_v = jnp.einsum("nbcy,nbcyz->nbcz", real_t, imag_f, precision=precise) + jnp.einsum("nbcy,nbcyz->nbcz", imag_t, real_f, precision=precise)
    return jnp.concatenate([real_v, imag_v], axis=-1).reshape(N_FACET * NBLK, N_CHAN, 2 * VIS)
```

```python
import functools
import math

import jax
import jax.numpy as jnp
import numpy as np
from jax import lax
from jax.experimental import pallas as pl
from jax.experimental.pallas import tpu as pltpu
from jax.sharding import PartitionSpec as P

FACET = 8192
SIDE = 8
SKY = 65536
WIN = 64
ROWS = 4
CAP = 2
LOW = 128
HIGH = FACET // LOW
COARSE = SKY // LOW
PARTS = 2 * ROWS
MESH = pl.DeviceIdType.MESH

precise = lax.Precision.HIGHEST


def turns(index, period):
    angle = 2.0 * np.pi * (index % period) / period
    return np.cos(angle), np.sin(angle)


def halves(table):
    high = table.astype(jnp.bfloat16)
    low = (table - high.astype(np.float64)).astype(jnp.bfloat16)
    return high, low


def tables(z_count, band_count):
    high_pos = np.arange(HIGH)
    low_pos = np.arange(LOW)
    coarse = np.arange(COARSE)
    cosines, sines = turns(high_pos[:, None] * coarse[None, :], COARSE)
    high, low = halves(np.concatenate([cosines, -sines], axis=1))
    outer = np.concatenate([high, high, low], axis=0)
    cosines, sines = turns(low_pos[:, None] * coarse[None, :], SKY)
    twiddle = np.concatenate([cosines, -sines], axis=1).astype(np.float32)
    cosines, sines = turns(np.arange(SIDE)[:, None] * coarse[None, :], SIDE)
    anchor = np.concatenate([cosines, -sines], axis=1).astype(np.float32)
    cosines, sines = turns(low_pos[:, None] * low_pos[None, :], LOW)
    full = np.concatenate(
        [
            np.concatenate([cosines, sines], axis=1),
            np.concatenate([-sines, cosines], axis=1),
        ],
        axis=0,
    )
    high, low = halves(full)
    inner = np.concatenate([high, high, low], axis=1)
    column = np.arange(PARTS * z_count)
    z_pos = column % z_count
    row_pos = (z_pos % SIDE) * FACET + (z_pos // SIDE) * ROWS + column // z_count // 2
    steps = np.arange(WIN)
    cosines, sines = turns(steps[:, None] * row_pos[None, :], SKY)
    scale = float((FACET * ROWS * band_count) ** -0.5) / WIN
    rows = scale * np.concatenate(
        [
            np.concatenate([cosines, -sines], axis=1),
            np.concatenate([sines, cosines], axis=1),
        ],
        axis=0,
    )
    cosines, sines = turns(steps[:, None] * steps[None, :], WIN)
    across = np.concatenate([cosines, sines], axis=1)
    across = np.concatenate([across] * CAP, axis=0)
    return (
        outer,
        twiddle,
        anchor,
        inner,
        rows.astype(np.float32),
        across.astype(np.float32),
    )


def kernel(
    z_count,
    x_count,
    half,
    owner,
    offset,
    tiles,
    coord,
    taylor,
    fourier,
    outer,
    twiddle,
    anchor,
    inner,
    rows,
    across,
    out,
    taylor_v,
    fourier_v,
    outer_v,
    twiddle_v,
    anchor_v,
    inner_v,
    rows_v,
    across_v,
    lhs,
    coarse_v,
    fine_v,
    freq,
    sent1,
    got1,
    sent2,
    got2,
    sent3,
    got3,
    sent4,
    got4,
    pick0,
    pick1,
    weights,
    load_sem,
    send1,
    recv1,
    send2,
    recv2,
    send3,
    recv3,
    send4,
    recv4,
):
    band = lax.axis_index("facet")
    x_pos = lax.axis_index("chan")
    z_pos = band // PARTS
    part = band % PARTS
    band_count = z_count * PARTS
    subs = 2 * half
    blocks = tiles.shape[0]

    barrier = pltpu.get_barrier_semaphore()
    peers1 = [(part + step) % PARTS for step in range(1, PARTS)]
    peers2 = [(x_pos + step) % x_count for step in range(1, x_count)]
    peers3 = [(z_pos + step) % z_count for step in range(1, z_count)]
    for peer in peers3:
        pl.semaphore_signal(barrier, inc=1, device_id=(peer * PARTS + part, x_pos), device_id_type=MESH)
    for peer in peers1:
        pl.semaphore_signal(barrier, inc=1, device_id=(z_pos * PARTS + peer, x_pos), device_id_type=MESH)
    for peer in peers2:
        pl.semaphore_signal(barrier, inc=1, device_id=(band, peer), device_id_type=MESH)

    loads = []
    for number, (source, target) in enumerate(
        [
            (taylor.at[0, 0], taylor_v),
            (outer, outer_v),
            (anchor, anchor_v),
            (twiddle, twiddle_v),
            (inner, inner_v),
            (rows, rows_v),
            (across, across_v),
            (fourier.at[:, 0], fourier_v),
        ]
    ):
        load = pltpu.make_async_copy(source, target, load_sem.at[number])
        load.start()
        loads.append(load)

    loads[0].wait()
    for high in range(HIGH):
        freq[0, pl.ds(high, ROWS, stride=HIGH), :] = taylor_v[:, high * LOW : (high + 1) * LOW]
    for row in range(ROWS):
        image = freq[0, row * HIGH : (row + 1) * HIGH, :]
        top = image.astype(jnp.bfloat16).astype(jnp.float32)
        stacked = jnp.concatenate([top, image - top, top], axis=0)
        lhs[row * LOW : (row + 1) * LOW, :] = jnp.transpose(stacked).astype(jnp.bfloat16)

    loads[1].wait()
    loads[2].wait()
    loads[3].wait()
    phase = anchor_v[pl.ds(part, 1), :]
    phase_r = phase[:, :COARSE]
    phase_i = phase[:, COARSE:]

    def turn_block(number, carry):
        place = pl.ds(pl.multiple_of(number * 16, 16), 16)
        real = twiddle_v[place, :COARSE]
        imag = twiddle_v[place, COARSE:]
        twiddle_v[place, :COARSE] = real * phase_r - imag * phase_i
        twiddle_v[place, COARSE:] = real * phase_i + imag * phase_r
        return carry

    lax.fori_loop(0, LOW // 16, turn_block, 0)

    loads[4].wait()
    for row in range(ROWS):
        coarse_v[...] = jnp.dot(
            lhs[row * LOW : (row + 1) * LOW, :], outer_v[...], preferred_element_type=jnp.float32
        )

        def fine_block(number, carry):
            start = pl.multiple_of(number * 16, 16)
            place = pl.ds(start, 16)
            real_c = coarse_v[place, :COARSE]
            imag_c = coarse_v[place, COARSE:]
            real_t = twiddle_v[place, :COARSE]
            imag_t = twiddle_v[place, COARSE:]
            real = real_c * real_t - imag_c * imag_t
            imag = real_c * imag_t + imag_c * real_t
            for shift, value in ((0, real), (LOW, imag)):
                top = value.astype(jnp.bfloat16)
                rest = (value - top.astype(jnp.float32)).astype(jnp.bfloat16)
                fine_v[pl.ds(start + shift, 16), :] = top
                fine_v[pl.ds(start + shift + 2 * LOW, 16), :] = rest
                fine_v[pl.ds(start + shift + 4 * LOW, 16), :] = top
            return carry

        lax.fori_loop(0, LOW // 16, fine_block, 0)
        result = jnp.dot(inner_v[...], fine_v[...], preferred_element_type=jnp.float32)
        for group in range(COARSE // LOW):
            freq[group, row * 2 * LOW : (row + 1) * 2 * LOW, :] = result[:, group * LOW : (group + 1) * LOW]

    lane = lax.broadcasted_iota(jnp.int32, (PARTS, LOW), 1)

    def pick(number, carry):
        found = []
        for side in range(2):
            start = offset[number + side * half, 0]
            shift = start % LOW
            first = start // LOW
            second = (first + 1) % (SKY // LOW)
            left = freq[first % 4, pl.ds(first // 4, PARTS, stride=LOW), :]
            right = freq[second % 4, pl.ds(second // 4, PARTS, stride=LOW), :]
            value = jnp.where(lane >= shift, left, right)
            found.append(pltpu.roll(value, (LOW + WIN * side - shift) % LOW, 1))
        sent1[pl.ds(number, PARTS, stride=half), :] = jnp.where(lane < WIN, found[0], found[1])
        return carry

    lax.fori_loop(0, half, pick, 0)

    pl.semaphore_wait(barrier, len(peers1) + len(peers2) + len(peers3))
    copies1 = []
    for step, peer in enumerate(peers1):
        copy = pltpu.make_async_remote_copy(
            src_ref=sent1.at[pl.ds(pl.multiple_of(peer * half, half), half), :],
            dst_ref=got1.at[step],
            send_sem=send1.at[step],
            recv_sem=recv1.at[step],
            device_id=(z_pos * PARTS + peer, x_pos),
            device_id_type=MESH,
        )
        copy.start()
        copies1.append(copy)

    lanes = lax.broadcasted_iota(jnp.int32, (8, subs), 1)
    plain = jnp.zeros((8, subs), jnp.int32)
    swapped = jnp.zeros((8, subs), jnp.int32)
    freq_v = [jnp.int32(0), jnp.int32(0)]
    seen = jnp.int32(0)
    for sub in range(subs):
        holder = owner[sub]
        plain = jnp.where(lanes == sub, holder, plain)
        swapped = jnp.where(lanes == (sub + half) % subs, holder, swapped)
        own = holder == band
        freq_v[0] = jnp.where(own & (seen == 0), offset[sub, 1], freq_v[0])
        freq_v[1] = jnp.where(own & (seen == 1), offset[sub, 1], freq_v[1])
        seen = seen + own.astype(jnp.int32)
    grid_row = lax.broadcasted_iota(jnp.int32, (subs, subs), 0)
    grid_col = lax.broadcasted_iota(jnp.int32, (subs, subs), 1)
    plain_f = plain[:1].astype(jnp.float32)
    swapped_f = swapped[:1].astype(jnp.float32)
    along = jnp.sum(jnp.where(grid_row == grid_col, plain_f, 0.0), axis=1, keepdims=True)
    place = lax.broadcasted_iota(jnp.int32, (band_count, subs), 0).astype(jnp.float32)
    for target, holders, number, wanted in (
        (pick0, plain_f, grid_col, 0.0),
        (pick1, swapped_f, (grid_col + half) % subs, 1.0),
    ):
        same = jnp.where((along == holders) & (grid_row < number), 1.0, 0.0)
        rank = jnp.sum(same, axis=0, keepdims=True)
        target[...] = jnp.where((place == holders) & (rank == wanted), 1.0, 0.0)

    wide = lax.broadcasted_iota(jnp.int32, (blocks, LOW), 1)
    deep = lax.broadcasted_iota(jnp.int32, (blocks, LOW), 0)
    tile = jnp.zeros((blocks, LOW), jnp.int32)
    for block in range(blocks):
        tile = jnp.where(deep == block, tiles[block], tile)
    clipped = jnp.maximum(tile, 0)
    tile_row = clipped % WIN
    tile_slot = clipped // WIN
    angle = (2.0 * math.pi / WIN) * ((wide % WIN * tile_row) % WIN).astype(jnp.float32)
    angle = jnp.where(wide < WIN, angle, angle - 0.5 * math.pi)
    loads[5].wait()
    sums = jnp.dot(jnp.cos(angle), rows_v[...], precision=precise, preferred_element_type=jnp.float32)
    span = PARTS * z_count
    column = lax.broadcasted_iota(jnp.int32, (blocks, span), 1)
    column_z = column % z_count
    column_part = column // z_count
    row_pos = column_z % SIDE * FACET + column_z // SIDE * ROWS + column_part // 2
    slot_v = jnp.where(tile_slot[:, :1] == 0, freq_v[0], freq_v[1])
    angle = (2.0 * math.pi / SKY) * ((slot_v * row_pos) & (SKY - 1)).astype(jnp.float32)
    cosines = jnp.cos(angle)
    sines = jnp.sin(angle)
    real = sums[:, :span] * cosines + sums[:, span:] * sines
    imag = sums[:, span:] * cosines - sums[:, :span] * sines
    usable = tile[:, :1] >= 0
    real = jnp.where(usable, real, 0.0)
    imag = jnp.where(usable, imag, 0.0)
    even = column_part % 2 == 0
    weights[:blocks, :] = jnp.where(even, real, -imag)
    weights[blocks:, :] = jnp.where(even, imag, real)

    total = sent1[pl.ds(pl.multiple_of(part * half, half), half), :]
    for step, copy in enumerate(copies1):
        copy.wait_recv()
        total = total + got1[step]
    sent2[...] = total

    copies2 = []
    for step, peer in enumerate(peers2):
        copy = pltpu.make_async_remote_copy(
            src_ref=sent2,
            dst_ref=got2.at[step],
            send_sem=send2.at[step],
            recv_sem=recv2.at[step],
            device_id=(band, peer),
            device_id_type=MESH,
        )
        copy.start()
        copies2.append(copy)
    here = coord[x_pos]

    def power(term):
        value = jnp.float32(1.0)
        product = jnp.float32(1.0)
        for degree in range(1, x_count):
            product = product * here
            value = jnp.where(term == degree, product, value)
        return value

    mixed = power(x_pos) * total
    for step, copy in enumerate(copies2):
        copy.wait_recv()
        mixed = mixed + power((x_pos + x_count - step - 1) % x_count) * got2[step]

    pair = jnp.concatenate([mixed, pltpu.roll(mixed, WIN, 1)], axis=0)
    slot0 = jnp.dot(pick0[...], pair, precision=precise, preferred_element_type=jnp.float32)
    slot1 = jnp.dot(pick1[...], pair, precision=precise, preferred_element_type=jnp.float32)
    slot_lane = lax.broadcasted_iota(jnp.int32, (band_count, LOW), 1)
    sent3[...] = jnp.where(slot_lane < WIN, slot0, slot1)
    own_z = pl.ds(pl.multiple_of(z_pos * PARTS, PARTS), PARTS)
    copies3 = []
    for step, peer in enumerate(peers3):
        copy = pltpu.make_async_remote_copy(
            src_ref=sent3.at[pl.ds(pl.multiple_of(peer * PARTS, PARTS), PARTS), :],
            dst_ref=got3.at[own_z, :],
            send_sem=send3.at[step],
            recv_sem=recv3.at[step],
            device_id=(peer * PARTS + part, x_pos),
            device_id_type=MESH,
        )
        copy.start()
        copies3.append(copy)
    got3[own_z, :] = sent3[own_z, :]
    for step in range(1, z_count):
        source = (z_pos + z_count - step) % z_count
        pltpu.make_async_remote_copy(
            src_ref=sent3.at[own_z, :],
            dst_ref=got3.at[pl.ds(pl.multiple_of(source * PARTS, PARTS), PARTS), :],
            send_sem=send3.at[step - 1],
            recv_sem=recv3.at[step - 1],
            device_id=(source * PARTS + part, x_pos),
            device_id_type=MESH,
        ).wait_recv()
    for peer in range(PARTS):
        sent4[peer * z_count : (peer + 1) * z_count, :] = got3[pl.ds(peer, z_count, stride=PARTS), :]
    own_part = pl.ds(pl.multiple_of(part * z_count, z_count), z_count)
    copies4 = []
    for step, peer in enumerate(peers1):
        copy = pltpu.make_async_remote_copy(
            src_ref=sent4.at[pl.ds(pl.multiple_of(peer * z_count, z_count), z_count), :],
            dst_ref=got4.at[own_part, :],
            send_sem=send4.at[step],
            recv_sem=recv4.at[step],
            device_id=(z_pos * PARTS + peer, x_pos),
            device_id_type=MESH,
        )
        copy.start()
        copies4.append(copy)
    got4[own_part, :] = sent4[own_part, :]
    for step in range(1, PARTS):
        source = (part + PARTS - step) % PARTS
        pltpu.make_async_remote_copy(
            src_ref=sent4.at[own_part, :],
            dst_ref=got4.at[pl.ds(pl.multiple_of(source * z_count, z_count), z_count), :],
            send_sem=send4.at[step - 1],
            recv_sem=recv4.at[step - 1],
            device_id=(z_pos * PARTS + source, x_pos),
            device_id_type=MESH,
        ).wait_recv()

    loads[6].wait()
    loads[7].wait()
    lines = jnp.dot(weights[...], got4[...], precision=precise, preferred_element_type=jnp.float32)
    keep = wide // WIN == tile_slot
    lines = jnp.where(jnp.concatenate([keep, keep], axis=0), lines, 0.0)
    spread = jnp.dot(lines, across_v[...], precision=precise, preferred_element_type=jnp.float32)
    crossed = pltpu.roll(spread[blocks:], WIN, 1)
    tile_rows = spread[:blocks] + jnp.where(wide < WIN, -crossed, crossed)
    upright = jnp.transpose(tile_rows)
    for block in range(blocks):
        real_t = upright[:WIN, block : block + 1]
        imag_t = upright[WIN:, block : block + 1]
        real_f = fourier_v[block, :, :LOW]
        imag_f = fourier_v[block, :, LOW:]
        out[block : block + 1, :LOW] = jnp.sum(real_t * real_f - imag_t * imag_f, axis=0, keepdims=True)
        out[block : block + 1, LOW:] = jnp.sum(real_t * imag_f + imag_t * real_f, axis=0, keepdims=True)

    for copy in copies1 + copies2 + copies3 + copies4:
        copy.wait_send()


def local(z_count, x_count, taylor, chan_coord, sub_offset, sub_owner, tile_list, fourier):
    constants = tables(z_count, z_count * PARTS)
    half = sub_owner.shape[0] // 2
    blocks = tile_list.shape[0]
    band_count = z_count * PARTS
    scratch = [
        pltpu.VMEM((ROWS, FACET), jnp.float32),
        pltpu.VMEM((blocks, WIN, 2 * LOW), jnp.float32),
    ]
    scratch += [pltpu.VMEM(table.shape, table.dtype) for table in constants]
    scratch += [
        pltpu.VMEM((ROWS * LOW, 3 * HIGH), jnp.bfloat16),
        pltpu.VMEM((LOW, 2 * COARSE), jnp.float32),
        pltpu.VMEM((6 * LOW, COARSE), jnp.bfloat16),
        pltpu.VMEM((COARSE // LOW, PARTS * LOW, LOW), jnp.float32),
        pltpu.VMEM((PARTS * half, LOW), jnp.float32),
        pltpu.VMEM((PARTS - 1, half, LOW), jnp.float32),
        pltpu.VMEM((half, LOW), jnp.float32),
        pltpu.VMEM((max(x_count - 1, 1), half, LOW), jnp.float32),
        pltpu.VMEM((band_count, LOW), jnp.float32),
        pltpu.VMEM((band_count, LOW), jnp.float32),
        pltpu.VMEM((band_count, LOW), jnp.float32),
        pltpu.VMEM((band_count, LOW), jnp.float32),
        pltpu.VMEM((band_count, 2 * half), jnp.float32),
        pltpu.VMEM((band_count, 2 * half), jnp.float32),
        pltpu.VMEM((2 * blocks, band_count), jnp.float32),
        pltpu.SemaphoreType.DMA((8,)),
    ]
    for count in (PARTS, max(x_count, 2), max(z_count, 2), PARTS):
        scratch += [pltpu.SemaphoreType.DMA((count - 1,))] * 2
    small = pl.BlockSpec(memory_space=pltpu.SMEM)
    large = pl.BlockSpec(memory_space=pl.ANY)
    visibilities = pl.pallas_call(
        functools.partial(kernel, z_count, x_count, half),
        out_shape=jax.ShapeDtypeStruct((blocks, 2 * LOW), jnp.float32),
        in_specs=[small] * 4 + [large] * (2 + len(constants)),
        out_specs=pl.BlockSpec(memory_space=pltpu.VMEM),
        scratch_shapes=scratch,
        compiler_params=pltpu.CompilerParams(collective_id=0, has_side_effects=True),
    )(sub_owner, sub_offset, tile_list, chan_coord, taylor, fourier, *[jnp.asarray(table) for table in constants])
    return visibilities[:, None, :]


def solution(mesh):
    return jax.shard_map(
        functools.partial(local, mesh.shape["facet"] // PARTS, mesh.shape["chan"]),
        mesh=mesh,
        in_specs=(
            P("facet", "chan", None, None),
            P(),
            P(),
            P(),
            P("facet"),
            P("facet", "chan", None, None),
        ),
        out_specs=P("facet", "chan", None),
        check_vma=False,
    )
```

```python
import functools
import math

import jax
import jax.numpy as jnp
import numpy as np
from jax import lax
from jax.experimental import pallas as pl
from jax.experimental.pallas import tpu as pltpu
from jax.sharding import PartitionSpec as P

FACET = 8192
SIDE = 8
SKY = 65536
WIN = 64
ROWS = 4
CAP = 2
LOW = 128
HIGH = FACET // LOW
COARSE = SKY // LOW
PARTS = 2 * ROWS
MESH = pl.DeviceIdType.MESH

precise = lax.Precision.HIGHEST


def turns(index, period):
    angle = 2.0 * np.pi * (index % period) / period
    return np.cos(angle), np.sin(angle)


def halves(table):
    high = table.astype(jnp.bfloat16)
    low = (table - high.astype(np.float64)).astype(jnp.bfloat16)
    return high, low


def tables(z_count, band_count):
    low_pos = np.arange(LOW)
    coarse = np.arange(COARSE)
    high_pos = np.arange(SIDE * HIGH)
    cosines, sines = turns(high_pos[:, None] * coarse[None, :], COARSE)
    outer = np.stack(halves(np.concatenate([cosines, -sines], axis=1)))
    cosines, sines = turns(low_pos[:, None] * coarse[None, :], SKY)
    twiddle = np.concatenate([cosines, -sines], axis=1).astype(np.float32)
    cosines, sines = turns(low_pos[:, None] * low_pos[None, :], LOW)
    full = np.concatenate(
        [
            np.concatenate([cosines, sines], axis=1),
            np.concatenate([-sines, cosines], axis=1),
        ],
        axis=0,
    )
    inner = np.stack(halves(full))
    column = np.arange(PARTS * z_count)
    z_pos = column // PARTS
    row_pos = (z_pos % SIDE) * FACET + (z_pos // SIDE) * ROWS + column % PARTS // 2
    steps = np.arange(WIN)
    cosines, sines = turns(steps[:, None] * row_pos[None, :], SKY)
    scale = float((FACET * ROWS * band_count) ** -0.5) / WIN
    rows = scale * np.concatenate(
        [
            np.concatenate([cosines, -sines], axis=1),
            np.concatenate([sines, cosines], axis=1),
        ],
        axis=0,
    )
    cosines, sines = turns(steps[:, None] * steps[None, :], WIN)
    across = np.concatenate([cosines, sines], axis=1)
    across = np.concatenate([across] * CAP, axis=0)
    return (
        outer,
        twiddle,
        inner,
        rows.astype(np.float32),
        across.astype(np.float32),
    )


def kernel(
    z_count,
    x_count,
    half,
    owner_h,
    offset_h,
    tiles_h,
    coord_h,
    taylor,
    fourier,
    outer,
    twiddle,
    inner,
    rows,
    across,
    out,
    owner,
    offset,
    tiles,
    coord,
    taylor_v,
    fourier_v,
    outer_v,
    twiddle_v,
    inner_v,
    rows_v,
    across_v,
    lhs,
    coarse_v,
    fine_v,
    freq,
    sent1,
    got1,
    sent2,
    got2,
    sent3,
    got3,
    pick0,
    pick1,
    weights,
    load_sem,
    send1,
    recv1,
    send2,
    recv2,
    send3,
    recv3,
):
    band = lax.axis_index("facet")
    x_pos = lax.axis_index("chan")
    z_pos = band // PARTS
    part = band % PARTS
    band_count = z_count * PARTS
    subs = 2 * half
    blocks = tiles.shape[0]

    loads = []
    for number, (source, target) in enumerate(
        [
            (taylor.at[0, 0], taylor_v),
            (outer.at[0, pl.ds(pl.multiple_of(part * HIGH, HIGH), HIGH), :], outer_v.at[:HIGH, :]),
            (outer.at[0, pl.ds(pl.multiple_of(part * HIGH, HIGH), HIGH), :], outer_v.at[HIGH : 2 * HIGH, :]),
            (outer.at[1, pl.ds(pl.multiple_of(part * HIGH, HIGH), HIGH), :], outer_v.at[2 * HIGH :, :]),
            (twiddle, twiddle_v),
            (inner.at[0], inner_v.at[:, : 2 * LOW]),
            (inner.at[0], inner_v.at[:, 2 * LOW : 4 * LOW]),
            (inner.at[1], inner_v.at[:, 4 * LOW :]),
            (offset_h, offset),
            (owner_h, owner),
            (tiles_h, tiles),
            (coord_h, coord),
            (rows, rows_v),
            (across, across_v),
            (fourier.at[:, 0], fourier_v),
        ]
    ):
        load = pltpu.make_async_copy(source, target, load_sem.at[number])
        load.start()
        loads.append(load)

    def wrapped(place, step, count):
        moved = place + step
        return jnp.where(moved >= count, moved - count, moved)

    barrier = pltpu.get_barrier_semaphore()
    far = sorted(range(z_count), key=lambda step: -min(step, z_count - step))
    peers_x = [wrapped(x_pos, step, x_count) for step in range(1, x_count)]
    parts = [wrapped(part, step, PARTS) for step in range(PARTS)]
    peers1 = [z_pos * PARTS + peer for peer in parts[1:]]
    peers3 = []
    for step in far:
        base = wrapped(z_pos, step, z_count) * PARTS
        peers3 += [base + peer for peer in (parts if step else parts[1:])]
    greeted = [wrapped(z_pos, step, z_count) * PARTS + part for step in far if step] + peers1
    for peer in greeted:
        pl.semaphore_signal(barrier, inc=1, device_id=(peer, x_pos), device_id_type=MESH)
    for peer in peers_x:
        pl.semaphore_signal(barrier, inc=1, device_id=(band, peer), device_id_type=MESH)

    loads[0].wait()
    for high in range(HIGH):
        freq[0, pl.ds(high, ROWS, stride=HIGH), :] = taylor_v[:, high * LOW : (high + 1) * LOW]
    for row in range(ROWS):
        image = freq[0, row * HIGH : (row + 1) * HIGH, :]
        top = image.astype(jnp.bfloat16).astype(jnp.float32)
        stacked = jnp.concatenate([top, image - top, top], axis=0)
        lhs[row * LOW : (row + 1) * LOW, :] = jnp.transpose(stacked).astype(jnp.bfloat16)

    for load in loads[1:8]:
        load.wait()
    for row in range(ROWS):
        coarse_v[row] = jnp.dot(
            lhs[row * LOW : (row + 1) * LOW, :], outer_v[...], preferred_element_type=jnp.float32
        )
        for start in range(0, LOW, 16):
            real_c = coarse_v[row, start : start + 16, :COARSE]
            imag_c = coarse_v[row, start : start + 16, COARSE:]
            real_t = twiddle_v[start : start + 16, :COARSE]
            imag_t = twiddle_v[start : start + 16, COARSE:]
            real = real_c * real_t - imag_c * imag_t
            imag = real_c * imag_t + imag_c * real_t
            for shift, value in ((start, real), (start + LOW, imag)):
                top = value.astype(jnp.bfloat16)
                rest = (value - top.astype(jnp.float32)).astype(jnp.bfloat16)
                fine_v[row, shift : shift + 16, :] = top
                fine_v[row, shift + 2 * LOW : shift + 2 * LOW + 16, :] = rest
                fine_v[row, shift + 4 * LOW : shift + 4 * LOW + 16, :] = top
        result = jnp.dot(inner_v[...], fine_v[row], preferred_element_type=jnp.float32)
        for group in range(COARSE // LOW):
            freq[group, row * 2 * LOW : (row + 1) * 2 * LOW, :] = result[:, group * LOW : (group + 1) * LOW]

    for load in loads[8:12]:
        load.wait()
    lane = lax.broadcasted_iota(jnp.int32, (PARTS, LOW), 1)
    bunch = min(8, half)

    def pick(number, carry):
        found = []
        for place in range(bunch):
            for side in range(2):
                start = offset[0, number * bunch + place + side * half]
                shift = start & (LOW - 1)
                first = lax.shift_right_logical(start, 7)
                second = (first + 1) & (SKY // LOW - 1)
                left = freq[first & 3, pl.ds(lax.shift_right_logical(first, 2), PARTS, stride=LOW), :]
                right = freq[second & 3, pl.ds(lax.shift_right_logical(second, 2), PARTS, stride=LOW), :]
                value = jnp.where(lane >= shift, left, right)
                found.append(pltpu.roll(value, (LOW + WIN * side - shift) & (LOW - 1), 1))
        for place in range(bunch):
            value = jnp.where(lane < WIN, found[2 * place], found[2 * place + 1])
            sent1[pl.ds(number * bunch + place, PARTS, stride=half), :] = value
        return carry

    lax.fori_loop(0, half // bunch, pick, 0)

    pl.semaphore_wait(barrier, len(peers_x) + len(greeted))
    copies1 = []
    for step, peer in enumerate(peers1):
        copy = pltpu.make_async_remote_copy(
            src_ref=sent1.at[pl.ds(pl.multiple_of(parts[step + 1] * half, half), half), :],
            dst_ref=got1.at[step],
            send_sem=send1.at[step],
            recv_sem=recv1.at[step],
            device_id=(peer, x_pos),
            device_id_type=MESH,
        )
        copy.start()
        copies1.append(copy)

    lanes = lax.broadcasted_iota(jnp.int32, (8, subs), 1)
    plain = jnp.zeros((8, subs), jnp.int32)
    swapped = jnp.zeros((8, subs), jnp.int32)
    freq_v = [jnp.int32(0), jnp.int32(0)]
    seen = jnp.int32(0)
    for sub in range(subs):
        holder = owner[sub]
        plain = jnp.where(lanes == sub, holder, plain)
        swapped = jnp.where(lanes == (sub + half) % subs, holder, swapped)
        own = holder == band
        freq_v[0] = jnp.where(own & (seen == 0), offset[1, sub], freq_v[0])
        freq_v[1] = jnp.where(own & (seen == 1), offset[1, sub], freq_v[1])
        seen = seen + own.astype(jnp.int32)
    grid_row = lax.broadcasted_iota(jnp.int32, (subs, subs), 0)
    grid_col = lax.broadcasted_iota(jnp.int32, (subs, subs), 1)
    plain_f = plain[:1].astype(jnp.float32)
    swapped_f = swapped[:1].astype(jnp.float32)
    along = jnp.sum(jnp.where(grid_row == grid_col, plain_f, 0.0), axis=1, keepdims=True)
    place = lax.broadcasted_iota(jnp.int32, (band_count, subs), 0).astype(jnp.float32)
    for target, holders, number, wanted in (
        (pick0, plain_f, grid_col, 0.0),
        (pick1, swapped_f, (grid_col + half) % subs, 1.0),
    ):
        same = jnp.where((along == holders) & (grid_row < number), 1.0, 0.0)
        rank = jnp.sum(same, axis=0, keepdims=True)
        target[...] = jnp.where((place == holders) & (rank == wanted), 1.0, 0.0)

    total = sent1[pl.ds(pl.multiple_of(part * half, half), half), :]
    for step, copy in enumerate(copies1):
        copy.wait_recv()
        total = total + got1[step]
    sent2[...] = total

    copies2 = []
    for step, peer in enumerate(peers_x):
        copy = pltpu.make_async_remote_copy(
            src_ref=sent2,
            dst_ref=got2.at[step],
            send_sem=send2.at[step],
            recv_sem=recv2.at[step],
            device_id=(band, peer),
            device_id_type=MESH,
        )
        copy.start()
        copies2.append(copy)
    here = coord[x_pos]

    def power(term):
        value = jnp.float32(1.0)
        product = jnp.float32(1.0)
        for degree in range(1, x_count):
            product = product * here
            value = jnp.where(term == degree, product, value)
        return value

    mixed = power(x_pos) * total
    for step, copy in enumerate(copies2):
        copy.wait_recv()
        mixed = mixed + power((x_pos + x_count - step - 1) % x_count) * got2[step]

    pair = jnp.concatenate([mixed, pltpu.roll(mixed, WIN, 1)], axis=0)
    slot0 = jnp.dot(pick0[...], pair, precision=precise, preferred_element_type=jnp.float32)
    slot1 = jnp.dot(pick1[...], pair, precision=precise, preferred_element_type=jnp.float32)
    slot_lane = lax.broadcasted_iota(jnp.int32, (band_count, LOW), 1)
    sent3[...] = jnp.where(slot_lane < WIN, slot0, slot1)
    own = pl.ds(band, 1)
    for peer in peers3:
        pltpu.make_async_remote_copy(
            src_ref=sent3.at[pl.ds(peer, 1), :],
            dst_ref=got3.at[own, :],
            send_sem=send3,
            recv_sem=recv3,
            device_id=(peer, x_pos),
            device_id_type=MESH,
        ).start()
    got3[own, :] = sent3[own, :]

    wide = lax.broadcasted_iota(jnp.int32, (blocks, LOW), 1)
    deep = lax.broadcasted_iota(jnp.int32, (blocks, LOW), 0)
    tile = jnp.zeros((blocks, LOW), jnp.int32)
    for block in range(blocks):
        tile = jnp.where(deep == block, tiles[block], tile)
    clipped = jnp.maximum(tile, 0)
    tile_row = clipped % WIN
    tile_slot = clipped // WIN
    angle = (2.0 * math.pi / WIN) * ((wide % WIN * tile_row) % WIN).astype(jnp.float32)
    angle = jnp.where(wide < WIN, angle, angle - 0.5 * math.pi)
    loads[12].wait()
    sums = jnp.dot(jnp.cos(angle), rows_v[...], precision=precise, preferred_element_type=jnp.float32)
    span = PARTS * z_count
    column = lax.broadcasted_iota(jnp.int32, (blocks, span), 1)
    column_z = column // PARTS
    column_part = column % PARTS
    row_pos = column_z % SIDE * FACET + column_z // SIDE * ROWS + column_part // 2
    slot_v = jnp.where(tile_slot[:, :1] == 0, freq_v[0], freq_v[1])
    angle = (2.0 * math.pi / SKY) * ((slot_v * row_pos) & (SKY - 1)).astype(jnp.float32)
    cosines = jnp.cos(angle)
    sines = jnp.sin(angle)
    real = sums[:, :span] * cosines + sums[:, span:] * sines
    imag = sums[:, span:] * cosines - sums[:, :span] * sines
    usable = tile[:, :1] >= 0
    real = jnp.where(usable, real, 0.0)
    imag = jnp.where(usable, imag, 0.0)
    even = column_part % 2 == 0
    weights[:blocks, :] = jnp.where(even, real, -imag)
    weights[blocks:, :] = jnp.where(even, imag, real)

    everyone = pltpu.make_async_copy(
        sent3.at[: len(peers3), :], got3.at[: len(peers3), :], recv3
    )
    everyone.wait()

    loads[13].wait()
    loads[14].wait()
    lines = jnp.dot(weights[...], got3[...], precision=precise, preferred_element_type=jnp.float32)
    keep = wide // WIN == tile_slot
    lines = jnp.where(jnp.concatenate([keep, keep], axis=0), lines, 0.0)
    spread = jnp.dot(lines, across_v[...], precision=precise, preferred_element_type=jnp.float32)
    crossed = pltpu.roll(spread[blocks:], WIN, 1)
    tile_rows = spread[:blocks] + jnp.where(wide < WIN, -crossed, crossed)
    upright = jnp.transpose(tile_rows)
    for block in range(blocks):
        real_t = upright[:WIN, block : block + 1]
        imag_t = upright[WIN:, block : block + 1]
        real_f = fourier_v[block, :, :LOW]
        imag_f = fourier_v[block, :, LOW:]
        out[block : block + 1, :LOW] = jnp.sum(real_t * real_f - imag_t * imag_f, axis=0, keepdims=True)
        out[block : block + 1, LOW:] = jnp.sum(real_t * imag_f + imag_t * real_f, axis=0, keepdims=True)

    for copy in copies1 + copies2:
        copy.wait_send()
    pltpu.make_async_copy(
        sent3.at[: len(peers3), :], got3.at[: len(peers3), :], send3
    ).wait()


def local(z_count, x_count, taylor, chan_coord, sub_offset, sub_owner, tile_list, fourier):
    constants = tables(z_count, z_count * PARTS)
    half = sub_owner.shape[0] // 2
    blocks = tile_list.shape[0]
    band_count = z_count * PARTS
    outer, twiddle, inner, rows, across = constants
    scratch = [
        pltpu.SMEM(sub_owner.shape, jnp.int32),
        pltpu.SMEM(sub_offset.shape[::-1], jnp.int32),
        pltpu.SMEM(tile_list.shape, jnp.int32),
        pltpu.SMEM(chan_coord.shape, jnp.float32),
        pltpu.VMEM((ROWS, FACET), jnp.float32),
        pltpu.VMEM((blocks, WIN, 2 * LOW), jnp.float32),
        pltpu.VMEM((3 * HIGH, 2 * COARSE), jnp.bfloat16),
        pltpu.VMEM(twiddle.shape, jnp.float32),
        pltpu.VMEM((2 * LOW, 6 * LOW), jnp.bfloat16),
        pltpu.VMEM(rows.shape, jnp.float32),
        pltpu.VMEM(across.shape, jnp.float32),
    ]
    scratch += [
        pltpu.VMEM((ROWS * LOW, 3 * HIGH), jnp.bfloat16),
        pltpu.VMEM((ROWS, LOW, 2 * COARSE), jnp.float32),
        pltpu.VMEM((ROWS, 6 * LOW, COARSE), jnp.bfloat16),
        pltpu.VMEM((COARSE // LOW, PARTS * LOW, LOW), jnp.float32),
        pltpu.VMEM((PARTS * half, LOW), jnp.float32),
        pltpu.VMEM((PARTS - 1, half, LOW), jnp.float32),
        pltpu.VMEM((half, LOW), jnp.float32),
        pltpu.VMEM((max(x_count - 1, 1), half, LOW), jnp.float32),
        pltpu.VMEM((band_count, LOW), jnp.float32),
        pltpu.VMEM((band_count, LOW), jnp.float32),
        pltpu.VMEM((band_count, 2 * half), jnp.float32),
        pltpu.VMEM((band_count, 2 * half), jnp.float32),
        pltpu.VMEM((2 * blocks, band_count), jnp.float32),
        pltpu.SemaphoreType.DMA((15,)),
    ]
    for count in (PARTS, max(x_count, 2)):
        scratch += [pltpu.SemaphoreType.DMA((count - 1,))] * 2
    scratch += [pltpu.SemaphoreType.DMA] * 2
    large = pl.BlockSpec(memory_space=pl.ANY)
    visibilities = pl.pallas_call(
        functools.partial(kernel, z_count, x_count, half),
        out_shape=jax.ShapeDtypeStruct((blocks, 2 * LOW), jnp.float32),
        in_specs=[large] * (6 + len(constants)),
        out_specs=pl.BlockSpec(memory_space=pltpu.VMEM),
        scratch_shapes=scratch,
        compiler_params=pltpu.CompilerParams(collective_id=0, has_side_effects=True),
    )(sub_owner, sub_offset.T, tile_list, chan_coord, taylor, fourier, *[jnp.asarray(table) for table in constants])
    return visibilities[:, None, :]


def solution(mesh):
    return jax.shard_map(
        functools.partial(local, mesh.shape["facet"] // PARTS, mesh.shape["chan"]),
        mesh=mesh,
        in_specs=(
            P("facet", "chan", None, None),
            P(),
            P(),
            P(),
            P("facet"),
            P("facet", "chan", None, None),
        ),
        out_specs=P("facet", "chan", None),
        check_vma=False,
    )
```

```python
import functools
import math

import jax
import jax.numpy as jnp
import numpy as np
from jax import lax
from jax.experimental import pallas as pl
from jax.experimental.pallas import tpu as pltpu
from jax.sharding import PartitionSpec as P

FACET = 8192
SIDE = 8
SKY = 65536
WIN = 64
ROWS = 4
CAP = 2
LOW = 128
HIGH = FACET // LOW
COARSE = SKY // LOW
SPAN = COARSE + LOW
PARTS = 2 * ROWS
MESH = pl.DeviceIdType.MESH

precise = lax.Precision.HIGHEST


def turns(index, period):
    angle = 2.0 * np.pi * (index % period) / period
    return np.cos(angle), np.sin(angle)


def halves(table):
    high = table.astype(jnp.bfloat16)
    low = (table - high.astype(np.float64)).astype(jnp.bfloat16)
    return high, low


def tables(z_count, band_count):
    low_pos = np.arange(LOW)
    coarse = np.arange(COARSE)
    high_pos = np.arange(SIDE * HIGH)
    cosines, sines = turns(high_pos[:, None] * coarse[None, :], COARSE)
    outer = np.stack(halves(np.concatenate([cosines, -sines], axis=1)))
    cosines, sines = turns(low_pos[:, None] * np.arange(SPAN)[None, :], SKY)
    twiddle = np.concatenate([cosines, -sines], axis=1).astype(np.float32)
    cosines, sines = turns(low_pos[:, None] * low_pos[None, :], LOW)
    inner = np.concatenate(halves(cosines) + halves(sines), axis=1)
    column = np.arange(PARTS * z_count)
    z_pos = column // PARTS
    row_pos = (z_pos % SIDE) * FACET + (z_pos // SIDE) * ROWS + column % PARTS // 2
    steps = np.arange(WIN)
    cosines, sines = turns(steps[:, None] * row_pos[None, :], SKY)
    scale = float((FACET * ROWS * band_count) ** -0.5) / WIN
    rows = scale * np.concatenate(
        [
            np.concatenate([cosines, -sines], axis=1),
            np.concatenate([sines, cosines], axis=1),
        ],
        axis=0,
    )
    cosines, sines = turns(steps[:, None] * steps[None, :], WIN)
    across = np.concatenate(
        [
            np.concatenate([cosines, -sines], axis=1),
            np.concatenate([sines, cosines], axis=1),
        ],
        axis=0,
    )
    high, low = halves(across)
    across = np.concatenate([high, high, low], axis=1)
    return (
        outer,
        twiddle,
        inner,
        rows.astype(np.float32),
        across,
    )


def kernel(
    z_count,
    x_count,
    half,
    owner_h,
    offset_h,
    tiles_h,
    coord_h,
    taylor,
    fourier,
    outer,
    twiddle,
    inner,
    rows,
    across,
    out,
    owner,
    offset,
    tiles,
    coord,
    taylor_v,
    fourier_v,
    outer_v,
    twiddle_v,
    inner_v,
    rows_v,
    across_v,
    offset_v,
    staged,
    lhs,
    lines_v,
    coarse_v,
    fine_v,
    spread_v,
    sent1,
    got1,
    sent2,
    got2,
    sent3,
    got3,
    picks,
    weights,
    load_sem,
    send1,
    recv1,
    send2,
    recv2,
    send3,
    recv3,
):
    band = lax.axis_index("facet")
    x_pos = lax.axis_index("chan")
    z_pos = band // PARTS
    part = band % PARTS
    band_count = z_count * PARTS
    subs = 2 * half
    blocks = tiles.shape[0]

    loads = []
    for number, (source, target) in enumerate(
        [
            (taylor.at[0, 0], taylor_v),
            (outer.at[0, pl.ds(pl.multiple_of(part * HIGH, HIGH), HIGH), :], outer_v.at[:HIGH, :]),
            (outer.at[0, pl.ds(pl.multiple_of(part * HIGH, HIGH), HIGH), :], outer_v.at[HIGH : 2 * HIGH, :]),
            (outer.at[1, pl.ds(pl.multiple_of(part * HIGH, HIGH), HIGH), :], outer_v.at[2 * HIGH :, :]),
            (twiddle, twiddle_v),
            (offset_h, offset_v),
            (inner, inner_v),
            (offset_h, offset),
            (owner_h, owner),
            (tiles_h, tiles),
            (coord_h, coord),
            (rows, rows_v),
            (across, across_v),
            (fourier.at[:, 0], fourier_v),
        ]
    ):
        load = pltpu.make_async_copy(source, target, load_sem.at[number])
        load.start()
        loads.append(load)

    def wrapped(place, step, count):
        moved = place + step
        return jnp.where(moved >= count, moved - count, moved)

    barrier = pltpu.get_barrier_semaphore()
    far = sorted(range(z_count), key=lambda step: -min(step, z_count - step))
    peers_x = [wrapped(x_pos, step, x_count) for step in range(1, x_count)]
    parts = [wrapped(part, step, PARTS) for step in range(PARTS)]
    peers1 = [z_pos * PARTS + peer for peer in parts[1:]]
    peers3 = []
    for step in far:
        base = wrapped(z_pos, step, z_count) * PARTS
        peers3 += [base + peer for peer in (parts if step else parts[1:])]
    greeted = [wrapped(z_pos, step, z_count) * PARTS + part for step in far if step] + peers1
    for peer in greeted:
        pl.semaphore_signal(barrier, inc=1, device_id=(peer, x_pos), device_id_type=MESH)
    for peer in peers_x:
        pl.semaphore_signal(barrier, inc=1, device_id=(band, peer), device_id_type=MESH)

    loads[0].wait()
    for high in range(HIGH):
        staged[pl.ds(high, ROWS, stride=HIGH), :] = taylor_v[:, high * LOW : (high + 1) * LOW]
    for row in range(ROWS):
        image = staged[row * HIGH : (row + 1) * HIGH, :]
        top = image.astype(jnp.bfloat16).astype(jnp.float32)
        stacked = jnp.concatenate([top, image - top, top], axis=0)
        lhs[row * LOW : (row + 1) * LOW, :] = jnp.transpose(stacked).astype(jnp.bfloat16)

    loads[5].wait()
    loads[6].wait()
    grid_row = lax.broadcasted_iota(jnp.int32, (subs, subs), 0)
    grid_col = lax.broadcasted_iota(jnp.int32, (subs, subs), 1)
    diagonal = grid_row == grid_col
    start = jnp.where(diagonal, offset_v[0:1, :].astype(jnp.float32), 0.0)
    start = jnp.broadcast_to(jnp.sum(start, axis=1, keepdims=True), (subs, LOW)).astype(jnp.int32)
    lane = lax.broadcasted_iota(jnp.int32, (subs, LOW), 1)
    deep = lax.broadcasted_iota(jnp.int32, (subs, LOW), 0)
    shift = start & (LOW - 1)
    group_of = (lax.shift_right_logical(start, 7) & 3) + jnp.where(lane < shift, 1, 0)
    target = (lane + shift + jnp.where(deep >= half, WIN, 0)) & (LOW - 1)
    chosen = jnp.where(lax.shift_right_logical(start, 9) == lane, 1.0, 0.0).astype(jnp.bfloat16)
    lines = jnp.dot(chosen, inner_v[...], preferred_element_type=jnp.float32)
    cos_h, cos_l, sin_h, sin_l = [lines[:, part * LOW : (part + 1) * LOW] for part in range(4)]
    real_line = jnp.concatenate([cos_h, sin_h, cos_h, sin_h, cos_l, sin_l], axis=1)
    imag_line = jnp.concatenate([-sin_h, cos_h, -sin_h, cos_h, -sin_l, cos_l], axis=1)
    lines_v[:subs, :] = real_line.astype(jnp.bfloat16)
    lines_v[subs:, :] = imag_line.astype(jnp.bfloat16)

    for load in loads[1:5]:
        load.wait()

    def coarse(row):
        coarse_v[row] = jnp.dot(
            lhs[row * LOW : (row + 1) * LOW, :], outer_v[...], preferred_element_type=jnp.float32
        )

    def turn(row):
        for start in range(0, LOW, 16):
            real_c = coarse_v[row, start : start + 16, :COARSE]
            imag_c = coarse_v[row, start : start + 16, COARSE:]
            real_c = jnp.concatenate([real_c, real_c[:, :LOW]], axis=1)
            imag_c = jnp.concatenate([imag_c, imag_c[:, :LOW]], axis=1)
            real_t = twiddle_v[start : start + 16, :SPAN]
            imag_t = twiddle_v[start : start + 16, SPAN:]
            real = real_c * real_t - imag_c * imag_t
            imag = real_c * imag_t + imag_c * real_t
            for place, value in ((start, real), (start + LOW, imag)):
                top = value.astype(jnp.bfloat16)
                rest = (value - top.astype(jnp.float32)).astype(jnp.bfloat16)
                fine_v[row, place : place + 16, :] = top
                fine_v[row, place + 2 * LOW : place + 2 * LOW + 16, :] = rest
                fine_v[row, place + 4 * LOW : place + 4 * LOW + 16, :] = top

    def fine(row):
        result = jnp.dot(lines_v[...], fine_v[row], preferred_element_type=jnp.float32)
        for side in range(2):
            found = result[side * subs : (side + 1) * subs, :]
            value = found[:, :LOW]
            for group in range(1, SPAN // LOW):
                value = jnp.where(group_of == group, found[:, group * LOW : (group + 1) * LOW], value)
            value = jnp.take_along_axis(value, target, axis=1, mode="promise_in_bounds")
            place = (2 * row + side) * half
            sent1[place : place + half, :] = jnp.where(lane[:half] < WIN, value[:half], value[half:])

    coarse(0)
    for row in range(ROWS):
        if row + 1 < ROWS:
            coarse(row + 1)
        turn(row)
        if row:
            fine(row - 1)
    fine(ROWS - 1)
    for load in loads[7:11]:
        load.wait()

    pl.semaphore_wait(barrier, len(peers_x) + len(greeted))
    copies1 = []
    for step, peer in enumerate(peers1):
        copy = pltpu.make_async_remote_copy(
            src_ref=sent1.at[pl.ds(pl.multiple_of(parts[step + 1] * half, half), half), :],
            dst_ref=got1.at[step],
            send_sem=send1.at[step],
            recv_sem=recv1.at[step],
            device_id=(peer, x_pos),
            device_id_type=MESH,
        )
        copy.start()
        copies1.append(copy)

    lanes = lax.broadcasted_iota(jnp.int32, (8, subs), 1)
    plain = jnp.zeros((8, subs), jnp.int32)
    swapped = jnp.zeros((8, subs), jnp.int32)
    freq_v = [jnp.int32(0), jnp.int32(0)]
    seen = jnp.int32(0)
    for sub in range(subs):
        holder = owner[sub]
        plain = jnp.where(lanes == sub, holder, plain)
        swapped = jnp.where(lanes == (sub + half) % subs, holder, swapped)
        own = holder == band
        freq_v[0] = jnp.where(own & (seen == 0), offset[1, sub], freq_v[0])
        freq_v[1] = jnp.where(own & (seen == 1), offset[1, sub], freq_v[1])
        seen = seen + own.astype(jnp.int32)
    plain_f = plain[:1].astype(jnp.float32)
    swapped_f = swapped[:1].astype(jnp.float32)
    along = jnp.sum(jnp.where(diagonal, plain_f, 0.0), axis=1, keepdims=True)
    place = lax.broadcasted_iota(jnp.int32, (band_count, subs), 0).astype(jnp.float32)
    for holders, number, wanted in (
        (plain_f, grid_col, 0.0),
        (swapped_f, (grid_col + half) % subs, 1.0),
    ):
        same = jnp.where((along == holders) & (grid_row < number), 1.0, 0.0)
        rank = jnp.sum(same, axis=0, keepdims=True)
        value = jnp.where((place == holders) & (rank == wanted), 1.0, 0.0)
        first = 2 * subs * int(wanted)
        picks[:, first : first + 2 * subs] = jnp.concatenate([value, value], axis=1).astype(jnp.bfloat16)

    total = sent1[pl.ds(pl.multiple_of(part * half, half), half), :]
    for step, copy in enumerate(copies1):
        copy.wait_recv()
        total = total + got1[step]
    sent2[...] = total

    copies2 = []
    for step, peer in enumerate(peers_x):
        copy = pltpu.make_async_remote_copy(
            src_ref=sent2,
            dst_ref=got2.at[step],
            send_sem=send2.at[step],
            recv_sem=recv2.at[step],
            device_id=(band, peer),
            device_id_type=MESH,
        )
        copy.start()
        copies2.append(copy)
    here = coord[x_pos]

    def power(term):
        value = jnp.float32(1.0)
        product = jnp.float32(1.0)
        for degree in range(1, x_count):
            product = product * here
            value = jnp.where(term == degree, product, value)
        return value

    mixed = power(x_pos) * total
    for step, copy in enumerate(copies2):
        copy.wait_recv()
        mixed = mixed + power((x_pos + x_count - step - 1) % x_count) * got2[step]

    pair = jnp.concatenate([mixed, pltpu.roll(mixed, WIN, 1)], axis=0)
    top = pair.astype(jnp.bfloat16).astype(jnp.float32)
    terms = jnp.concatenate([top, pair - top], axis=0)
    side = lax.broadcasted_iota(jnp.int32, (2 * subs, LOW), 1) < WIN
    terms = jnp.concatenate([jnp.where(side, terms, 0.0), jnp.where(side, 0.0, terms)], axis=0)
    sent3[...] = jnp.dot(picks[...], terms.astype(jnp.bfloat16), preferred_element_type=jnp.float32)
    own = pl.ds(band, 1)
    for peer in peers3:
        pltpu.make_async_remote_copy(
            src_ref=sent3.at[pl.ds(peer, 1), :],
            dst_ref=got3.at[own, :],
            send_sem=send3,
            recv_sem=recv3,
            device_id=(peer, x_pos),
            device_id_type=MESH,
        ).start()
    got3[own, :] = sent3[own, :]

    wide = lax.broadcasted_iota(jnp.int32, (blocks, LOW), 1)
    deep = lax.broadcasted_iota(jnp.int32, (blocks, LOW), 0)
    tile = jnp.zeros((blocks, LOW), jnp.int32)
    for block in range(blocks):
        tile = jnp.where(deep == block, tiles[block], tile)
    clipped = jnp.maximum(tile, 0)
    tile_row = clipped % WIN
    tile_slot = clipped // WIN
    angle = (2.0 * math.pi / WIN) * ((wide % WIN * tile_row) % WIN).astype(jnp.float32)
    angle = jnp.where(wide < WIN, angle, angle - 0.5 * math.pi)
    loads[11].wait()
    sums = jnp.dot(jnp.cos(angle), rows_v[...], precision=precise, preferred_element_type=jnp.float32)
    span = PARTS * z_count
    column = lax.broadcasted_iota(jnp.int32, (blocks, span), 1)
    column_z = column // PARTS
    column_part = column % PARTS
    row_pos = column_z % SIDE * FACET + column_z // SIDE * ROWS + column_part // 2
    slot_v = jnp.where(tile_slot[:, :1] == 0, freq_v[0], freq_v[1])
    angle = (2.0 * math.pi / SKY) * ((slot_v * row_pos) & (SKY - 1)).astype(jnp.float32)
    cosines = jnp.cos(angle)
    sines = jnp.sin(angle)
    real = sums[:, :span] * cosines + sums[:, span:] * sines
    imag = sums[:, span:] * cosines - sums[:, :span] * sines
    usable = tile[:, :1] >= 0
    real = jnp.where(usable, real, 0.0)
    imag = jnp.where(usable, imag, 0.0)
    even = column_part % 2 == 0
    for first, value in ((0, jnp.where(even, real, -imag)), (blocks, jnp.where(even, imag, real))):
        top = value.astype(jnp.bfloat16)
        rest = (value - top.astype(jnp.float32)).astype(jnp.bfloat16)
        weights[first : first + blocks, :span] = top
        weights[first : first + blocks, span : 2 * span] = top
        weights[first : first + blocks, 2 * span :] = rest

    loads[12].wait()
    loads[13].wait()
    for block in range(0, blocks, 2):
        value = jnp.concatenate(
            [
                jnp.concatenate([fourier_v[block, :, :LOW], fourier_v[block, :, LOW:]], axis=0),
                jnp.concatenate([fourier_v[block + 1, :, :LOW], fourier_v[block + 1, :, LOW:]], axis=0),
            ],
            axis=1,
        )
        top = value.astype(jnp.bfloat16)
        rest = (value - top.astype(jnp.float32)).astype(jnp.bfloat16)
        stacked = jnp.concatenate([top, rest, top], axis=0)
        spread_v[block // 2] = jnp.dot(across_v[...], stacked, preferred_element_type=jnp.float32)

    everyone = pltpu.make_async_copy(
        sent3.at[: len(peers3), :], got3.at[: len(peers3), :], recv3
    )
    everyone.wait()

    value = got3[...]
    top = value.astype(jnp.bfloat16)
    rest = (value - top.astype(jnp.float32)).astype(jnp.bfloat16)
    stacked = jnp.concatenate([top, rest, top], axis=0)
    lines = jnp.dot(weights[...], stacked, preferred_element_type=jnp.float32)
    first_slot = jnp.concatenate([tile_slot, tile_slot], axis=0) == 0
    lines = jnp.where(first_slot, lines, pltpu.roll(lines, WIN, 1))
    upright = jnp.transpose(lines)
    for block in range(blocks):
        real_t = upright[:WIN, block : block + 1]
        imag_t = upright[:WIN, blocks + block : blocks + block + 1]
        place = block % 2 * LOW
        real_f = spread_v[block // 2, :WIN, place : place + LOW]
        imag_f = spread_v[block // 2, WIN:, place : place + LOW]
        out[block : block + 1, :LOW] = jnp.sum(real_t * real_f - imag_t * imag_f, axis=0, keepdims=True)
        out[block : block + 1, LOW:] = jnp.sum(real_t * imag_f + imag_t * real_f, axis=0, keepdims=True)

    for copy in copies1 + copies2:
        copy.wait_send()
    pltpu.make_async_copy(
        sent3.at[: len(peers3), :], got3.at[: len(peers3), :], send3
    ).wait()


def local(z_count, x_count, taylor, chan_coord, sub_offset, sub_owner, tile_list, fourier):
    constants = tables(z_count, z_count * PARTS)
    half = sub_owner.shape[0] // 2
    blocks = tile_list.shape[0]
    band_count = z_count * PARTS
    outer, twiddle, inner, rows, across = constants
    scratch = [
        pltpu.SMEM(sub_owner.shape, jnp.int32),
        pltpu.SMEM(sub_offset.shape[::-1], jnp.int32),
        pltpu.SMEM(tile_list.shape, jnp.int32),
        pltpu.SMEM(chan_coord.shape, jnp.float32),
        pltpu.VMEM((ROWS, FACET), jnp.float32),
        pltpu.VMEM((blocks, WIN, 2 * LOW), jnp.float32),
        pltpu.VMEM((3 * HIGH, 2 * COARSE), jnp.bfloat16),
        pltpu.VMEM(twiddle.shape, jnp.float32),
        pltpu.VMEM(inner.shape, jnp.bfloat16),
        pltpu.VMEM(rows.shape, jnp.float32),
        pltpu.VMEM(across.shape, jnp.bfloat16),
        pltpu.VMEM(sub_offset.shape[::-1], jnp.int32),
        pltpu.VMEM((ROWS * HIGH, LOW), jnp.float32),
    ]
    scratch += [
        pltpu.VMEM((ROWS * LOW, 3 * HIGH), jnp.bfloat16),
        pltpu.VMEM((4 * half, 6 * LOW), jnp.bfloat16),
        pltpu.VMEM((ROWS, LOW, 2 * COARSE), jnp.float32),
        pltpu.VMEM((ROWS, 6 * LOW, SPAN), jnp.bfloat16),
        pltpu.VMEM((blocks // 2, 2 * WIN, 2 * LOW), jnp.float32),
        pltpu.VMEM((PARTS * half, LOW), jnp.float32),
        pltpu.VMEM((PARTS - 1, half, LOW), jnp.float32),
        pltpu.VMEM((half, LOW), jnp.float32),
        pltpu.VMEM((max(x_count - 1, 1), half, LOW), jnp.float32),
        pltpu.VMEM((band_count, LOW), jnp.float32),
        pltpu.VMEM((band_count, LOW), jnp.float32),
        pltpu.VMEM((band_count, 8 * half), jnp.bfloat16),
        pltpu.VMEM((2 * blocks, 3 * band_count), jnp.bfloat16),
        pltpu.SemaphoreType.DMA((14,)),
    ]
    for count in (PARTS, max(x_count, 2)):
        scratch += [pltpu.SemaphoreType.DMA((count - 1,))] * 2
    scratch += [pltpu.SemaphoreType.DMA] * 2
    large = pl.BlockSpec(memory_space=pl.ANY)
    visibilities = pl.pallas_call(
        functools.partial(kernel, z_count, x_count, half),
        out_shape=jax.ShapeDtypeStruct((blocks, 2 * LOW), jnp.float32),
        in_specs=[large] * (6 + len(constants)),
        out_specs=pl.BlockSpec(memory_space=pltpu.VMEM),
        scratch_shapes=scratch,
        compiler_params=pltpu.CompilerParams(collective_id=0, has_side_effects=True),
    )(sub_owner, sub_offset.T, tile_list, chan_coord, taylor, fourier, *[jnp.asarray(table) for table in constants])
    return visibilities[:, None, :]


def solution(mesh):
    return jax.shard_map(
        functools.partial(local, mesh.shape["facet"] // PARTS, mesh.shape["chan"]),
        mesh=mesh,
        in_specs=(
            P("facet", "chan", None, None),
            P(),
            P(),
            P(),
            P("facet"),
            P("facet", "chan", None, None),
        ),
        out_specs=P("facet", "chan", None),
        check_vma=False,
    )
```

```python
import functools
import math

import jax
import jax.numpy as jnp
import numpy as np
from jax import lax
from jax.experimental import pallas as pl
from jax.experimental.pallas import tpu as pltpu
from jax.sharding import PartitionSpec as P

FACET = 8192
SIDE = 8
SKY = 65536
WIN = 64
ROWS = 4
CAP = 2
LOW = 128
HIGH = FACET // LOW
COARSE = SKY // LOW
SPAN = COARSE + LOW
PARTS = 2 * ROWS
MESH = pl.DeviceIdType.MESH

precise = lax.Precision.HIGHEST


def turns(index, period):
    angle = 2.0 * np.pi * (index % period) / period
    return np.cos(angle), np.sin(angle)


def halves(table):
    high = table.astype(jnp.bfloat16)
    low = (table - high.astype(np.float64)).astype(jnp.bfloat16)
    return high, low


def tables(z_count, band_count):
    low_pos = np.arange(LOW)
    coarse = np.arange(COARSE)
    high_pos = np.arange(SIDE * HIGH)
    cosines, sines = turns(high_pos[:, None] * coarse[None, :], COARSE)
    outer = np.stack(halves(np.concatenate([cosines, -sines], axis=1)))
    cosines, sines = turns(low_pos[:, None] * np.arange(SPAN)[None, :], SKY)
    twiddle = np.concatenate([cosines, -sines], axis=1).astype(np.float32)
    cosines, sines = turns(low_pos[:, None] * low_pos[None, :], LOW)
    inner = np.concatenate(halves(cosines) + halves(sines), axis=1)
    column = np.arange(PARTS * z_count)
    z_pos = column // PARTS
    row_pos = (z_pos % SIDE) * FACET + (z_pos // SIDE) * ROWS + column % PARTS // 2
    steps = np.arange(WIN)
    cosines, sines = turns(steps[:, None] * row_pos[None, :], SKY)
    scale = float((FACET * ROWS * band_count) ** -0.5) / WIN
    rows = scale * np.concatenate(
        [
            np.concatenate([cosines, -sines], axis=1),
            np.concatenate([sines, cosines], axis=1),
        ],
        axis=0,
    )
    cosines, sines = turns(steps[:, None] * steps[None, :], WIN)
    across = np.concatenate(
        [
            np.concatenate([cosines, -sines], axis=1),
            np.concatenate([sines, cosines], axis=1),
        ],
        axis=0,
    )
    high, low = halves(across)
    across = np.concatenate([high, high, low], axis=1)
    return (
        outer,
        twiddle,
        inner,
        rows.astype(np.float32),
        across,
    )


def kernel(
    z_count,
    x_count,
    half,
    owner_h,
    offset_h,
    tiles_h,
    coord_h,
    taylor,
    fourier,
    outer,
    twiddle,
    inner,
    rows,
    across,
    out,
    owner,
    offset,
    tiles,
    coord,
    taylor_v,
    fourier_v,
    outer_v,
    twiddle_v,
    inner_v,
    rows_v,
    across_v,
    offset_v,
    staged,
    lhs,
    lines_v,
    coarse_v,
    fine_v,
    spread_v,
    sent1,
    got1,
    sent2,
    got2,
    sent3,
    got3,
    picks,
    weights,
    load_sem,
    send1,
    recv1,
    send2,
    recv2,
    send3,
    recv3,
):
    band = lax.axis_index("facet")
    x_pos = lax.axis_index("chan")
    z_pos = band // PARTS
    part = band % PARTS
    band_count = z_count * PARTS
    subs = 2 * half
    blocks = tiles.shape[0]

    loads = []
    for number, (source, target) in enumerate(
        [
            (taylor.at[0, 0], taylor_v),
            (outer.at[0, pl.ds(pl.multiple_of(part * HIGH, HIGH), HIGH), :], outer_v.at[:HIGH, :]),
            (outer.at[0, pl.ds(pl.multiple_of(part * HIGH, HIGH), HIGH), :], outer_v.at[HIGH : 2 * HIGH, :]),
            (outer.at[1, pl.ds(pl.multiple_of(part * HIGH, HIGH), HIGH), :], outer_v.at[2 * HIGH :, :]),
            (twiddle, twiddle_v),
            (offset_h, offset_v),
            (inner, inner_v),
            (offset_h, offset),
            (owner_h, owner),
            (tiles_h, tiles),
            (coord_h, coord),
            (rows, rows_v),
            (across, across_v),
            (fourier.at[:, 0], fourier_v),
        ]
    ):
        load = pltpu.make_async_copy(source, target, load_sem.at[number])
        load.start()
        loads.append(load)

    def wrapped(place, step, count):
        moved = place + step
        return jnp.where(moved >= count, moved - count, moved)

    barrier = pltpu.get_barrier_semaphore()
    far = sorted(range(z_count), key=lambda step: -min(step, z_count - step))
    peers_x = [wrapped(x_pos, step, x_count) for step in range(1, x_count)]
    parts = [wrapped(part, step, PARTS) for step in range(PARTS)]
    peers1 = [z_pos * PARTS + peer for peer in parts[1:]]
    peers3 = []
    for step in far:
        base = wrapped(z_pos, step, z_count) * PARTS
        peers3 += [base + peer for peer in (parts if step else parts[1:])]
    greeted = [wrapped(z_pos, step, z_count) * PARTS + part for step in far if step] + peers1
    for peer in greeted:
        pl.semaphore_signal(barrier, inc=1, device_id=(peer, x_pos), device_id_type=MESH)
    for peer in peers_x:
        pl.semaphore_signal(barrier, inc=1, device_id=(band, peer), device_id_type=MESH)

    loads[0].wait()
    for high in range(HIGH):
        staged[pl.ds(high, ROWS, stride=HIGH), :] = taylor_v[:, high * LOW : (high + 1) * LOW]
    for row in range(ROWS):
        image = staged[row * HIGH : (row + 1) * HIGH, :]
        top = image.astype(jnp.bfloat16).astype(jnp.float32)
        stacked = jnp.concatenate([top, image - top, top], axis=0)
        lhs[row * LOW : (row + 1) * LOW, :] = jnp.transpose(stacked).astype(jnp.bfloat16)

    loads[5].wait()
    loads[6].wait()
    grid_row = lax.broadcasted_iota(jnp.int32, (subs, subs), 0)
    grid_col = lax.broadcasted_iota(jnp.int32, (subs, subs), 1)
    diagonal = grid_row == grid_col
    start = jnp.where(diagonal, offset_v[0:1, :].astype(jnp.float32), 0.0)
    start = jnp.broadcast_to(jnp.sum(start, axis=1, keepdims=True), (subs, LOW)).astype(jnp.int32)
    lane = lax.broadcasted_iota(jnp.int32, (subs, LOW), 1)
    deep = lax.broadcasted_iota(jnp.int32, (subs, LOW), 0)
    shift = start & (LOW - 1)
    group_of = (lax.shift_right_logical(start, 7) & 3) + jnp.where(lane < shift, 1, 0)
    target = (lane + shift + jnp.where(deep >= half, WIN, 0)) & (LOW - 1)
    chosen = jnp.where(lax.shift_right_logical(start, 9) == lane, 1.0, 0.0).astype(jnp.bfloat16)
    lines = jnp.dot(chosen, inner_v[...], preferred_element_type=jnp.float32)
    cos_h, cos_l, sin_h, sin_l = [lines[:, part * LOW : (part + 1) * LOW] for part in range(4)]
    real_line = jnp.concatenate([cos_h, sin_h, cos_h, sin_h, cos_l, sin_l], axis=1)
    imag_line = jnp.concatenate([-sin_h, cos_h, -sin_h, cos_h, -sin_l, cos_l], axis=1)
    lines_v[:subs, :] = real_line.astype(jnp.bfloat16)
    lines_v[subs:, :] = imag_line.astype(jnp.bfloat16)

    for load in loads[1:5]:
        load.wait()

    def coarse(row):
        coarse_v[row] = jnp.dot(
            lhs[row * LOW : (row + 1) * LOW, :], outer_v[...], preferred_element_type=jnp.float32
        )

    def turn(row):
        for start in range(0, LOW, 16):
            real_c = coarse_v[row, start : start + 16, :COARSE]
            imag_c = coarse_v[row, start : start + 16, COARSE:]
            real_c = jnp.concatenate([real_c, real_c[:, :LOW]], axis=1)
            imag_c = jnp.concatenate([imag_c, imag_c[:, :LOW]], axis=1)
            real_t = twiddle_v[start : start + 16, :SPAN]
            imag_t = twiddle_v[start : start + 16, SPAN:]
            real = real_c * real_t - imag_c * imag_t
            imag = real_c * imag_t + imag_c * real_t
            for place, value in ((start, real), (start + LOW, imag)):
                top = value.astype(jnp.bfloat16)
                rest = (value - top.astype(jnp.float32)).astype(jnp.bfloat16)
                fine_v[row, place : place + 16, :] = top
                fine_v[row, place + 2 * LOW : place + 2 * LOW + 16, :] = rest
                fine_v[row, place + 4 * LOW : place + 4 * LOW + 16, :] = top

    def fine(row):
        result = jnp.dot(lines_v[...], fine_v[row], preferred_element_type=jnp.float32)
        for side in range(2):
            found = result[side * subs : (side + 1) * subs, :]
            value = found[:, :LOW]
            for group in range(1, SPAN // LOW):
                value = jnp.where(group_of == group, found[:, group * LOW : (group + 1) * LOW], value)
            value = jnp.take_along_axis(value, target, axis=1, mode="promise_in_bounds")
            place = (2 * row + side) * half
            sent1[place : place + half, :] = jnp.where(lane[:half] < WIN, value[:half], value[half:])

    coarse(0)
    for row in range(ROWS):
        if row + 1 < ROWS:
            coarse(row + 1)
        turn(row)
        if row:
            fine(row - 1)
    fine(ROWS - 1)
    for load in loads[7:11]:
        load.wait()

    pl.semaphore_wait(barrier, len(peers_x) + len(greeted))
    copies1 = []
    for step, peer in enumerate(peers1):
        copy = pltpu.make_async_remote_copy(
            src_ref=sent1.at[pl.ds(pl.multiple_of(parts[step + 1] * half, half), half), :],
            dst_ref=got1.at[step],
            send_sem=send1.at[step],
            recv_sem=recv1.at[step],
            device_id=(peer, x_pos),
            device_id_type=MESH,
        )
        copy.start()
        copies1.append(copy)

    lanes = lax.broadcasted_iota(jnp.int32, (8, subs), 1)
    plain = jnp.zeros((8, subs), jnp.int32)
    swapped = jnp.zeros((8, subs), jnp.int32)
    freq_v = [jnp.int32(0), jnp.int32(0)]
    seen = jnp.int32(0)
    for sub in range(subs):
        holder = owner[sub]
        plain = jnp.where(lanes == sub, holder, plain)
        swapped = jnp.where(lanes == (sub + half) % subs, holder, swapped)
        own = holder == band
        freq_v[0] = jnp.where(own & (seen == 0), offset[1, sub], freq_v[0])
        freq_v[1] = jnp.where(own & (seen == 1), offset[1, sub], freq_v[1])
        seen = seen + own.astype(jnp.int32)
    plain_f = plain[:1].astype(jnp.float32)
    swapped_f = swapped[:1].astype(jnp.float32)
    along = jnp.sum(jnp.where(diagonal, plain_f, 0.0), axis=1, keepdims=True)
    place = lax.broadcasted_iota(jnp.int32, (band_count, subs), 0).astype(jnp.float32)
    for holders, number, wanted in (
        (plain_f, grid_col, 0.0),
        (swapped_f, (grid_col + half) % subs, 1.0),
    ):
        same = jnp.where((along == holders) & (grid_row < number), 1.0, 0.0)
        rank = jnp.sum(same, axis=0, keepdims=True)
        value = jnp.where((place == holders) & (rank == wanted), 1.0, 0.0)
        first = 2 * subs * int(wanted)
        picks[:, first : first + 2 * subs] = jnp.concatenate([value, value], axis=1).astype(jnp.bfloat16)

    total = sent1[pl.ds(pl.multiple_of(part * half, half), half), :]
    for step, copy in enumerate(copies1):
        copy.wait_recv()
        total = total + got1[step]
    sent2[...] = total

    copies2 = []
    for step, peer in enumerate(peers_x):
        copy = pltpu.make_async_remote_copy(
            src_ref=sent2,
            dst_ref=got2.at[step],
            send_sem=send2.at[step],
            recv_sem=recv2.at[step],
            device_id=(band, peer),
            device_id_type=MESH,
        )
        copy.start()
        copies2.append(copy)
    here = coord[x_pos]

    def power(term):
        value = jnp.float32(1.0)
        product = jnp.float32(1.0)
        for degree in range(1, x_count):
            product = product * here
            value = jnp.where(term == degree, product, value)
        return value

    mixed = power(x_pos) * total
    for step, copy in enumerate(copies2):
        copy.wait_recv()
        mixed = mixed + power((x_pos + x_count - step - 1) % x_count) * got2[step]

    pair = jnp.concatenate([mixed, pltpu.roll(mixed, WIN, 1)], axis=0)
    top = pair.astype(jnp.bfloat16).astype(jnp.float32)
    terms = jnp.concatenate([top, pair - top], axis=0)
    side = lax.broadcasted_iota(jnp.int32, (2 * subs, LOW), 1) < WIN
    terms = jnp.concatenate([jnp.where(side, terms, 0.0), jnp.where(side, 0.0, terms)], axis=0)
    sent3[...] = jnp.dot(picks[...], terms.astype(jnp.bfloat16), preferred_element_type=jnp.float32)
    own = pl.ds(band, 1)
    for peer in peers3:
        pltpu.make_async_remote_copy(
            src_ref=sent3.at[pl.ds(peer, 1), :],
            dst_ref=got3.at[own, :],
            send_sem=send3,
            recv_sem=recv3,
            device_id=(peer, x_pos),
            device_id_type=MESH,
        ).start()
    got3[own, :] = sent3[own, :]

    wide = lax.broadcasted_iota(jnp.int32, (blocks, LOW), 1)
    deep = lax.broadcasted_iota(jnp.int32, (blocks, LOW), 0)
    tile = jnp.zeros((blocks, LOW), jnp.int32)
    for block in range(blocks):
        tile = jnp.where(deep == block, tiles[block], tile)
    clipped = jnp.maximum(tile, 0)
    tile_row = clipped % WIN
    tile_slot = clipped // WIN
    angle = (2.0 * math.pi / WIN) * ((wide % WIN * tile_row) % WIN).astype(jnp.float32)
    angle = jnp.where(wide < WIN, angle, angle - 0.5 * math.pi)
    loads[11].wait()
    sums = jnp.dot(jnp.cos(angle), rows_v[...], precision=precise, preferred_element_type=jnp.float32)
    span = PARTS * z_count
    column = lax.broadcasted_iota(jnp.int32, (blocks, span), 1)
    column_z = column // PARTS
    column_part = column % PARTS
    row_pos = column_z % SIDE * FACET + column_z // SIDE * ROWS + column_part // 2
    slot_v = jnp.where(tile_slot[:, :1] == 0, freq_v[0], freq_v[1])
    angle = (2.0 * math.pi / SKY) * ((slot_v * row_pos) & (SKY - 1)).astype(jnp.float32)
    cosines = jnp.cos(angle)
    sines = jnp.sin(angle)
    real = sums[:, :span] * cosines + sums[:, span:] * sines
    imag = sums[:, span:] * cosines - sums[:, :span] * sines
    usable = tile[:, :1] >= 0
    real = jnp.where(usable, real, 0.0)
    imag = jnp.where(usable, imag, 0.0)
    even = column_part % 2 == 0
    for first, value in ((0, jnp.where(even, real, -imag)), (blocks, jnp.where(even, imag, real))):
        top = value.astype(jnp.bfloat16)
        rest = (value - top.astype(jnp.float32)).astype(jnp.bfloat16)
        weights[first : first + blocks, :span] = top
        weights[first : first + blocks, span : 2 * span] = top
        weights[first : first + blocks, 2 * span :] = rest

    loads[12].wait()
    loads[13].wait()
    for block in range(0, blocks, 2):
        value = jnp.concatenate(
            [
                jnp.concatenate([fourier_v[block, :, :LOW], fourier_v[block, :, LOW:]], axis=0),
                jnp.concatenate([fourier_v[block + 1, :, :LOW], fourier_v[block + 1, :, LOW:]], axis=0),
            ],
            axis=1,
        )
        top = value.astype(jnp.bfloat16)
        rest = (value - top.astype(jnp.float32)).astype(jnp.bfloat16)
        stacked = jnp.concatenate([top, rest, top], axis=0)
        spread_v[block // 2] = jnp.dot(across_v[...], stacked, preferred_element_type=jnp.float32)

    everyone = pltpu.make_async_copy(
        sent3.at[: len(peers3), :], got3.at[: len(peers3), :], recv3
    )
    everyone.wait()

    value = got3[...]
    top = value.astype(jnp.bfloat16)
    rest = (value - top.astype(jnp.float32)).astype(jnp.bfloat16)
    stacked = jnp.concatenate([top, rest, top], axis=0)
    lines = jnp.dot(weights[...], stacked, preferred_element_type=jnp.float32)
    first_slot = jnp.concatenate([tile_slot, tile_slot], axis=0) == 0
    lines = jnp.where(first_slot, lines, pltpu.roll(lines, WIN, 1))
    upright = jnp.transpose(lines)
    for block in range(blocks):
        real_t = upright[:WIN, block : block + 1]
        imag_t = upright[:WIN, blocks + block : blocks + block + 1]
        place = block % 2 * LOW
        real_f = spread_v[block // 2, :WIN, place : place + LOW]
        imag_f = spread_v[block // 2, WIN:, place : place + LOW]
        out[block : block + 1, :LOW] = jnp.sum(real_t * real_f - imag_t * imag_f, axis=0, keepdims=True)
        out[block : block + 1, LOW:] = jnp.sum(real_t * imag_f + imag_t * real_f, axis=0, keepdims=True)

    for copy in copies1 + copies2:
        copy.wait_send()
    pltpu.make_async_copy(
        sent3.at[: len(peers3), :], got3.at[: len(peers3), :], send3
    ).wait()


def local(z_count, x_count, taylor, chan_coord, sub_offset, sub_owner, tile_list, fourier):
    constants = tables(z_count, z_count * PARTS)
    half = sub_owner.shape[0] // 2
    blocks = tile_list.shape[0]
    band_count = z_count * PARTS
    outer, twiddle, inner, rows, across = constants
    scratch = [
        pltpu.SMEM(sub_owner.shape, jnp.int32),
        pltpu.SMEM(sub_offset.shape[::-1], jnp.int32),
        pltpu.SMEM(tile_list.shape, jnp.int32),
        pltpu.SMEM(chan_coord.shape, jnp.float32),
        pltpu.VMEM((ROWS, FACET), jnp.float32),
        pltpu.VMEM((blocks, WIN, 2 * LOW), jnp.float32),
        pltpu.VMEM((3 * HIGH, 2 * COARSE), jnp.bfloat16),
        pltpu.VMEM(twiddle.shape, jnp.float32),
        pltpu.VMEM(inner.shape, jnp.bfloat16),
        pltpu.VMEM(rows.shape, jnp.float32),
        pltpu.VMEM(across.shape, jnp.bfloat16),
        pltpu.VMEM(sub_offset.shape[::-1], jnp.int32),
        pltpu.VMEM((ROWS * HIGH, LOW), jnp.float32),
    ]
    scratch += [
        pltpu.VMEM((ROWS * LOW, 3 * HIGH), jnp.bfloat16),
        pltpu.VMEM((4 * half, 6 * LOW), jnp.bfloat16),
        pltpu.VMEM((ROWS, LOW, 2 * COARSE), jnp.float32),
        pltpu.VMEM((ROWS, 6 * LOW, SPAN), jnp.bfloat16),
        pltpu.VMEM((blocks // 2, 2 * WIN, 2 * LOW), jnp.float32),
        pltpu.VMEM((PARTS * half, LOW), jnp.float32),
        pltpu.VMEM((PARTS - 1, half, LOW), jnp.float32),
        pltpu.VMEM((half, LOW), jnp.float32),
        pltpu.VMEM((max(x_count - 1, 1), half, LOW), jnp.float32),
        pltpu.VMEM((band_count, LOW), jnp.float32),
        pltpu.VMEM((band_count, LOW), jnp.float32),
        pltpu.VMEM((band_count, 8 * half), jnp.bfloat16),
        pltpu.VMEM((2 * blocks, 3 * band_count), jnp.bfloat16),
        pltpu.SemaphoreType.DMA((14,)),
    ]
    for count in (PARTS, max(x_count, 2)):
        scratch += [pltpu.SemaphoreType.DMA((count - 1,))] * 2
    scratch += [pltpu.SemaphoreType.DMA] * 2
    large = pl.BlockSpec(memory_space=pl.ANY)
    visibilities = pl.pallas_call(
        functools.partial(kernel, z_count, x_count, half),
        out_shape=jax.ShapeDtypeStruct((blocks, 2 * LOW), jnp.float32),
        in_specs=[large] * (6 + len(constants)),
        out_specs=pl.BlockSpec(memory_space=pltpu.VMEM),
        scratch_shapes=scratch,
        compiler_params=pltpu.CompilerParams(collective_id=0, has_side_effects=True, vmem_limit_bytes=26 * 2**20),
    )(*[
        pltpu.with_memory_space_constraint(value, pltpu.HBM)
        for value in (sub_owner, sub_offset.T, tile_list, chan_coord, taylor, fourier, *[jnp.asarray(table) for table in constants])
    ])
    return visibilities[:, None, :]


def solution(mesh):
    return jax.shard_map(
        functools.partial(local, mesh.shape["facet"] // PARTS, mesh.shape["chan"]),
        mesh=mesh,
        in_specs=(
            P("facet", "chan", None, None),
            P(),
            P(),
            P(),
            P("facet"),
            P("facet", "chan", None, None),
        ),
        out_specs=P("facet", "chan", None),
        check_vma=False,
    )
```

```python
import functools
import math

import jax
import jax.numpy as jnp
import numpy as np
from jax import lax
from jax.experimental import pallas as pl
from jax.experimental.pallas import tpu as pltpu
from jax.sharding import PartitionSpec as P

FACET = 8192
SIDE = 8
SKY = 65536
WIN = 64
ROWS = 4
CAP = 2
LOW = 128
HIGH = FACET // LOW
COARSE = SKY // LOW
SPAN = COARSE + LOW
PARTS = 2 * ROWS
MESH = pl.DeviceIdType.MESH

precise = lax.Precision.HIGHEST


def turns(index, period):
    angle = 2.0 * np.pi * (index % period) / period
    return np.cos(angle), np.sin(angle)


def halves(table):
    high = table.astype(jnp.bfloat16)
    low = (table - high.astype(np.float64)).astype(jnp.bfloat16)
    return high, low


def tables(z_count, band_count):
    low_pos = np.arange(LOW)
    coarse = np.arange(COARSE)
    high_pos = np.arange(SIDE * HIGH)
    cosines, sines = turns(high_pos[:, None] * coarse[None, :], COARSE)
    outer = np.stack(halves(np.concatenate([cosines, -sines], axis=1)))
    rows = np.concatenate([16 * np.arange(LOW // 16), np.arange(16)])
    cosines, sines = turns(rows[:, None] * np.arange(SPAN)[None, :], SKY)
    twiddle = np.concatenate([cosines, -sines], axis=1).astype(np.float32)
    cosines, sines = turns(low_pos[:, None] * low_pos[None, :], LOW)
    inner = np.concatenate(halves(cosines) + halves(sines), axis=1)
    column = np.arange(PARTS * z_count)
    z_pos = column // PARTS
    row_pos = (z_pos % SIDE) * FACET + (z_pos // SIDE) * ROWS + column % PARTS // 2
    steps = np.arange(WIN)
    cosines, sines = turns(steps[:, None] * row_pos[None, :], SKY)
    scale = float((FACET * ROWS * band_count) ** -0.5) / WIN
    rows = scale * np.concatenate(
        [
            np.concatenate([cosines, -sines], axis=1),
            np.concatenate([sines, cosines], axis=1),
        ],
        axis=0,
    )
    cosines, sines = turns(steps[:, None] * steps[None, :], WIN)
    across = np.concatenate(
        [
            np.concatenate([cosines, -sines], axis=1),
            np.concatenate([sines, cosines], axis=1),
        ],
        axis=0,
    )
    high, low = halves(across)
    across = np.concatenate([high, high, low], axis=1)
    return (
        outer,
        twiddle,
        inner,
        rows.astype(np.float32),
        across,
    )


def kernel(
    z_count,
    x_count,
    half,
    owner_h,
    offset_h,
    tiles_h,
    coord_h,
    taylor,
    fourier,
    outer,
    twiddle,
    inner,
    rows,
    across,
    out,
    owner,
    offset,
    tiles,
    coord,
    taylor_v,
    fourier_v,
    outer_v,
    small_v,
    twiddle_v,
    inner_v,
    rows_v,
    across_v,
    offset_v,
    staged,
    lhs,
    lines_v,
    coarse_v,
    fine_v,
    spread_v,
    sent1,
    got1,
    sent2,
    got2,
    sent3,
    got3,
    picks,
    weights,
    load_sem,
    send1,
    recv1,
    send2,
    recv2,
    send3,
    recv3,
):
    band = lax.axis_index("facet")
    x_pos = lax.axis_index("chan")
    z_pos = band // PARTS
    part = band % PARTS
    band_count = z_count * PARTS
    subs = 2 * half
    blocks = tiles.shape[0]

    loads = []
    for number, (source, target) in enumerate(
        [
            (taylor.at[0, 0], taylor_v),
            (offset_h, offset_v),
            (twiddle, small_v),
            (outer.at[0, pl.ds(pl.multiple_of(part * HIGH, HIGH), HIGH), :], outer_v.at[:HIGH, :]),
            (outer.at[1, pl.ds(pl.multiple_of(part * HIGH, HIGH), HIGH), :], outer_v.at[HIGH:, :]),
            (inner, inner_v),
            (offset_h, offset),
            (owner_h, owner),
            (tiles_h, tiles),
            (coord_h, coord),
            (rows, rows_v),
            (across, across_v),
            (fourier.at[:, 0], fourier_v),
        ]
    ):
        load = pltpu.make_async_copy(source, target, load_sem.at[number])
        load.start()
        loads.append(load)

    def wrapped(place, step, count):
        moved = place + step
        return jnp.where(moved >= count, moved - count, moved)

    barrier = pltpu.get_barrier_semaphore()
    far = sorted(range(z_count), key=lambda step: -min(step, z_count - step))
    steps_x = sorted(range(1, x_count), key=lambda step: -min(step, x_count - step))
    steps1 = sorted(range(1, PARTS), key=lambda step: -min(step, PARTS - step))
    peers_x = [wrapped(x_pos, step, x_count) for step in steps_x]
    parts = [wrapped(part, step, PARTS) for step in range(PARTS)]
    peers1 = [z_pos * PARTS + parts[step] for step in steps1]
    peers3 = []
    for step in far:
        base = wrapped(z_pos, step, z_count) * PARTS
        peers3 += [base + peer for peer in (parts if step else parts[1:])]
    greeted = [wrapped(z_pos, step, z_count) * PARTS + part for step in far if step] + peers1
    for peer in greeted:
        pl.semaphore_signal(barrier, inc=1, device_id=(peer, x_pos), device_id_type=MESH)
    for peer in peers_x:
        pl.semaphore_signal(barrier, inc=1, device_id=(band, peer), device_id_type=MESH)

    loads[2].wait()
    for high in range(LOW // 16):
        for first in range(0, SPAN, LOW):
            real_h = small_v[high : high + 1, first : first + LOW]
            imag_h = small_v[high : high + 1, SPAN + first : SPAN + first + LOW]
            real_l = small_v[LOW // 16 :, first : first + LOW]
            imag_l = small_v[LOW // 16 :, SPAN + first : SPAN + first + LOW]
            place = slice(high * 16, high * 16 + 16)
            twiddle_v[place, first : first + LOW] = real_h * real_l - imag_h * imag_l
            twiddle_v[place, SPAN + first : SPAN + first + LOW] = real_h * imag_l + imag_h * real_l

    loads[0].wait()
    for high in range(HIGH):
        staged[pl.ds(high, ROWS, stride=HIGH), :] = taylor_v[:, high * LOW : (high + 1) * LOW]
    for row in range(ROWS):
        image = staged[row * HIGH : (row + 1) * HIGH, :]
        top = image.astype(jnp.bfloat16).astype(jnp.float32)
        stacked = jnp.concatenate([top, image - top, top], axis=0)
        lhs[row * LOW : (row + 1) * LOW, :] = jnp.transpose(stacked).astype(jnp.bfloat16)

    loads[1].wait()
    loads[5].wait()
    grid_row = lax.broadcasted_iota(jnp.int32, (subs, subs), 0)
    grid_col = lax.broadcasted_iota(jnp.int32, (subs, subs), 1)
    diagonal = grid_row == grid_col
    start = jnp.where(diagonal, offset_v[0:1, :].astype(jnp.float32), 0.0)
    start = jnp.broadcast_to(jnp.sum(start, axis=1, keepdims=True), (subs, LOW)).astype(jnp.int32)
    lane = lax.broadcasted_iota(jnp.int32, (subs, LOW), 1)
    deep = lax.broadcasted_iota(jnp.int32, (subs, LOW), 0)
    shift = start & (LOW - 1)
    group_of = (lax.shift_right_logical(start, 7) & 3) + jnp.where(lane < shift, 1, 0)
    target = (lane + shift + jnp.where(deep >= half, WIN, 0)) & (LOW - 1)
    chosen = jnp.where(lax.shift_right_logical(start, 9) == lane, 1.0, 0.0).astype(jnp.bfloat16)
    lines = jnp.dot(chosen, inner_v[...], preferred_element_type=jnp.float32)
    cos_h, cos_l, sin_h, sin_l = [lines[:, part * LOW : (part + 1) * LOW] for part in range(4)]
    real_line = jnp.concatenate([cos_h, sin_h, cos_h, sin_h, cos_l, sin_l], axis=1)
    imag_line = jnp.concatenate([-sin_h, cos_h, -sin_h, cos_h, -sin_l, cos_l], axis=1)
    lines_v[:subs, :] = real_line.astype(jnp.bfloat16)
    lines_v[subs:, :] = imag_line.astype(jnp.bfloat16)

    loads[3].wait()
    loads[4].wait()

    def coarse(row):
        top = outer_v[:HIGH, :]
        table = jnp.concatenate([top, top, outer_v[HIGH:, :]], axis=0)
        coarse_v[row] = jnp.dot(
            lhs[row * LOW : (row + 1) * LOW, :], table, preferred_element_type=jnp.float32
        )

    def turn(row):
        for start in range(0, LOW, 16):
            real_c = coarse_v[row, start : start + 16, :COARSE]
            imag_c = coarse_v[row, start : start + 16, COARSE:]
            real_c = jnp.concatenate([real_c, real_c[:, :LOW]], axis=1)
            imag_c = jnp.concatenate([imag_c, imag_c[:, :LOW]], axis=1)
            real_t = twiddle_v[start : start + 16, :SPAN]
            imag_t = twiddle_v[start : start + 16, SPAN:]
            real = real_c * real_t - imag_c * imag_t
            imag = real_c * imag_t + imag_c * real_t
            for place, value in ((start, real), (start + LOW, imag)):
                top = value.astype(jnp.bfloat16)
                rest = (value - top.astype(jnp.float32)).astype(jnp.bfloat16)
                fine_v[row, place : place + 16, :] = top
                fine_v[row, place + 2 * LOW : place + 2 * LOW + 16, :] = rest

    def fine(row):
        data = jnp.concatenate([fine_v[row], fine_v[row, : 2 * LOW, :]], axis=0)
        result = jnp.dot(lines_v[...], data, preferred_element_type=jnp.float32)
        for side in range(2):
            found = result[side * subs : (side + 1) * subs, :]
            value = found[:, :LOW]
            for group in range(1, SPAN // LOW):
                value = jnp.where(group_of == group, found[:, group * LOW : (group + 1) * LOW], value)
            value = jnp.take_along_axis(value, target, axis=1, mode="promise_in_bounds")
            place = (2 * row + side) * half
            sent1[place : place + half, :] = jnp.where(lane[:half] < WIN, value[:half], value[half:])

    coarse(0)
    for row in range(ROWS):
        if row + 1 < ROWS:
            coarse(row + 1)
        turn(row)
        if row:
            fine(row - 1)
    fine(ROWS - 1)
    for load in loads[6:10]:
        load.wait()

    pl.semaphore_wait(barrier, len(peers_x) + len(greeted))
    copies1 = []
    for step, peer in enumerate(peers1):
        copy = pltpu.make_async_remote_copy(
            src_ref=sent1.at[pl.ds(pl.multiple_of(parts[steps1[step]] * half, half), half), :],
            dst_ref=got1.at[step],
            send_sem=send1.at[step],
            recv_sem=recv1.at[step],
            device_id=(peer, x_pos),
            device_id_type=MESH,
        )
        copy.start()
        copies1.append(copy)

    lanes = lax.broadcasted_iota(jnp.int32, (8, subs), 1)
    plain = jnp.zeros((8, subs), jnp.int32)
    swapped = jnp.zeros((8, subs), jnp.int32)
    freq_v = [jnp.int32(0), jnp.int32(0)]
    seen = jnp.int32(0)
    for sub in range(subs):
        holder = owner[sub]
        plain = jnp.where(lanes == sub, holder, plain)
        swapped = jnp.where(lanes == (sub + half) % subs, holder, swapped)
        own = holder == band
        freq_v[0] = jnp.where(own & (seen == 0), offset[1, sub], freq_v[0])
        freq_v[1] = jnp.where(own & (seen == 1), offset[1, sub], freq_v[1])
        seen = seen + own.astype(jnp.int32)
    plain_f = plain[:1].astype(jnp.float32)
    swapped_f = swapped[:1].astype(jnp.float32)
    along = jnp.sum(jnp.where(diagonal, plain_f, 0.0), axis=1, keepdims=True)
    place = lax.broadcasted_iota(jnp.int32, (band_count, subs), 0).astype(jnp.float32)
    for holders, number, wanted in (
        (plain_f, grid_col, 0.0),
        (swapped_f, (grid_col + half) % subs, 1.0),
    ):
        same = jnp.where((along == holders) & (grid_row < number), 1.0, 0.0)
        rank = jnp.sum(same, axis=0, keepdims=True)
        value = jnp.where((place == holders) & (rank == wanted), 1.0, 0.0)
        first = 2 * subs * int(wanted)
        picks[:, first : first + 2 * subs] = jnp.concatenate([value, value], axis=1).astype(jnp.bfloat16)

    total = sent1[pl.ds(pl.multiple_of(part * half, half), half), :]
    for step, copy in enumerate(copies1):
        copy.wait_recv()
        total = total + got1[step]
    sent2[...] = total

    copies2 = []
    for step, peer in enumerate(peers_x):
        copy = pltpu.make_async_remote_copy(
            src_ref=sent2,
            dst_ref=got2.at[step],
            send_sem=send2.at[step],
            recv_sem=recv2.at[step],
            device_id=(band, peer),
            device_id_type=MESH,
        )
        copy.start()
        copies2.append(copy)
    here = coord[x_pos]

    def power(term):
        value = jnp.float32(1.0)
        product = jnp.float32(1.0)
        for degree in range(1, x_count):
            product = product * here
            value = jnp.where(term == degree, product, value)
        return value

    mixed = power(x_pos) * total
    for step, copy in enumerate(copies2):
        copy.wait_recv()
        mixed = mixed + power((x_pos + x_count - steps_x[step]) % x_count) * got2[step]

    pair = jnp.concatenate([mixed, pltpu.roll(mixed, WIN, 1)], axis=0)
    top = pair.astype(jnp.bfloat16).astype(jnp.float32)
    terms = jnp.concatenate([top, pair - top], axis=0)
    side = lax.broadcasted_iota(jnp.int32, (2 * subs, LOW), 1) < WIN
    terms = jnp.concatenate([jnp.where(side, terms, 0.0), jnp.where(side, 0.0, terms)], axis=0)
    sent3[...] = jnp.dot(picks[...], terms.astype(jnp.bfloat16), preferred_element_type=jnp.float32)
    own = pl.ds(band, 1)
    for peer in peers3:
        pltpu.make_async_remote_copy(
            src_ref=sent3.at[pl.ds(peer, 1), :],
            dst_ref=got3.at[own, :],
            send_sem=send3,
            recv_sem=recv3,
            device_id=(peer, x_pos),
            device_id_type=MESH,
        ).start()
    got3[own, :] = sent3[own, :]

    wide = lax.broadcasted_iota(jnp.int32, (blocks, LOW), 1)
    deep = lax.broadcasted_iota(jnp.int32, (blocks, LOW), 0)
    tile = jnp.zeros((blocks, LOW), jnp.int32)
    for block in range(blocks):
        tile = jnp.where(deep == block, tiles[block], tile)
    clipped = jnp.maximum(tile, 0)
    tile_row = clipped % WIN
    tile_slot = clipped // WIN
    angle = (2.0 * math.pi / WIN) * ((wide % WIN * tile_row) % WIN).astype(jnp.float32)
    angle = jnp.where(wide < WIN, angle, angle - 0.5 * math.pi)
    loads[10].wait()
    sums = jnp.dot(jnp.cos(angle), rows_v[...], precision=precise, preferred_element_type=jnp.float32)
    span = PARTS * z_count
    column = lax.broadcasted_iota(jnp.int32, (blocks, span), 1)
    column_z = column // PARTS
    column_part = column % PARTS
    row_pos = column_z % SIDE * FACET + column_z // SIDE * ROWS + column_part // 2
    slot_v = jnp.where(tile_slot[:, :1] == 0, freq_v[0], freq_v[1])
    angle = (2.0 * math.pi / SKY) * ((slot_v * row_pos) & (SKY - 1)).astype(jnp.float32)
    cosines = jnp.cos(angle)
    sines = jnp.sin(angle)
    real = sums[:, :span] * cosines + sums[:, span:] * sines
    imag = sums[:, span:] * cosines - sums[:, :span] * sines
    usable = tile[:, :1] >= 0
    real = jnp.where(usable, real, 0.0)
    imag = jnp.where(usable, imag, 0.0)
    even = column_part % 2 == 0
    for first, value in ((0, jnp.where(even, real, -imag)), (blocks, jnp.where(even, imag, real))):
        top = value.astype(jnp.bfloat16)
        rest = (value - top.astype(jnp.float32)).astype(jnp.bfloat16)
        weights[first : first + blocks, :span] = top
        weights[first : first + blocks, span : 2 * span] = top
        weights[first : first + blocks, 2 * span :] = rest

    loads[11].wait()
    loads[12].wait()
    for block in range(0, blocks, 2):
        value = jnp.concatenate(
            [
                jnp.concatenate([fourier_v[block, :, :LOW], fourier_v[block, :, LOW:]], axis=0),
                jnp.concatenate([fourier_v[block + 1, :, :LOW], fourier_v[block + 1, :, LOW:]], axis=0),
            ],
            axis=1,
        )
        top = value.astype(jnp.bfloat16)
        rest = (value - top.astype(jnp.float32)).astype(jnp.bfloat16)
        stacked = jnp.concatenate([top, rest, top], axis=0)
        spread = jnp.dot(across_v[...], stacked, preferred_element_type=jnp.float32)
        for side in range(2):
            real_f = spread[:WIN, side * LOW : (side + 1) * LOW]
            imag_f = spread[WIN:, side * LOW : (side + 1) * LOW]
            value = jnp.concatenate(
                [
                    jnp.concatenate([real_f, imag_f], axis=1),
                    jnp.concatenate([-imag_f, real_f], axis=1),
                ],
                axis=0,
            )
            top = value.astype(jnp.bfloat16)
            place = (block + side) * LOW
            spread_v[0, place : place + LOW, :] = top
            spread_v[1, place : place + LOW, :] = (value - top.astype(jnp.float32)).astype(jnp.bfloat16)

    everyone = pltpu.make_async_copy(
        sent3.at[: len(peers3), :], got3.at[: len(peers3), :], recv3
    )
    everyone.wait()

    value = got3[...]
    top = value.astype(jnp.bfloat16)
    rest = (value - top.astype(jnp.float32)).astype(jnp.bfloat16)
    stacked = jnp.concatenate([top, rest, top], axis=0)
    lines = jnp.dot(weights[...], stacked, preferred_element_type=jnp.float32)
    first_slot = jnp.concatenate([tile_slot, tile_slot], axis=0) == 0
    lines = jnp.where(first_slot, lines, pltpu.roll(lines, WIN, 1))
    value = jnp.where(wide < WIN, lines[:blocks], pltpu.roll(lines[blocks:], WIN, 1))
    top = value.astype(jnp.bfloat16).astype(jnp.float32)
    stacked = jnp.concatenate([top, value - top], axis=0)
    deep = lax.broadcasted_iota(jnp.int32, (2 * blocks, LOW), 0) % blocks
    spread = jnp.concatenate([jnp.where(deep == block, stacked, 0.0) for block in range(blocks)], axis=1)
    spread = spread.astype(jnp.bfloat16)
    result = jnp.dot(spread, spread_v[0], preferred_element_type=jnp.float32)
    rest = jnp.dot(spread[:blocks], spread_v[1], preferred_element_type=jnp.float32)
    out[...] = result[:blocks] + result[blocks:] + rest

    for copy in copies1 + copies2:
        copy.wait_send()
    pltpu.make_async_copy(
        sent3.at[: len(peers3), :], got3.at[: len(peers3), :], send3
    ).wait()


def local(z_count, x_count, taylor, chan_coord, sub_offset, sub_owner, tile_list, fourier):
    constants = tables(z_count, z_count * PARTS)
    half = sub_owner.shape[0] // 2
    blocks = tile_list.shape[0]
    band_count = z_count * PARTS
    outer, twiddle, inner, rows, across = constants
    scratch = [
        pltpu.SMEM(sub_owner.shape, jnp.int32),
        pltpu.SMEM(sub_offset.shape[::-1], jnp.int32),
        pltpu.SMEM(tile_list.shape, jnp.int32),
        pltpu.SMEM(chan_coord.shape, jnp.float32),
        pltpu.VMEM((ROWS, FACET), jnp.float32),
        pltpu.VMEM((blocks, WIN, 2 * LOW), jnp.float32),
        pltpu.VMEM((2 * HIGH, 2 * COARSE), jnp.bfloat16),
        pltpu.VMEM(twiddle.shape, jnp.float32),
        pltpu.VMEM((LOW, 2 * SPAN), jnp.float32),
        pltpu.VMEM(inner.shape, jnp.bfloat16),
        pltpu.VMEM(rows.shape, jnp.float32),
        pltpu.VMEM(across.shape, jnp.bfloat16),
        pltpu.VMEM(sub_offset.shape[::-1], jnp.int32),
        pltpu.VMEM((ROWS * HIGH, LOW), jnp.float32),
    ]
    scratch += [
        pltpu.VMEM((ROWS * LOW, 3 * HIGH), jnp.bfloat16),
        pltpu.VMEM((4 * half, 6 * LOW), jnp.bfloat16),
        pltpu.VMEM((ROWS, LOW, 2 * COARSE), jnp.float32),
        pltpu.VMEM((ROWS, 4 * LOW, SPAN), jnp.bfloat16),
        pltpu.VMEM((2, blocks * LOW, 2 * LOW), jnp.bfloat16),
        pltpu.VMEM((PARTS * half, LOW), jnp.float32),
        pltpu.VMEM((PARTS - 1, half, LOW), jnp.float32),
        pltpu.VMEM((half, LOW), jnp.float32),
        pltpu.VMEM((max(x_count - 1, 1), half, LOW), jnp.float32),
        pltpu.VMEM((band_count, LOW), jnp.float32),
        pltpu.VMEM((band_count, LOW), jnp.float32),
        pltpu.VMEM((band_count, 8 * half), jnp.bfloat16),
        pltpu.VMEM((2 * blocks, 3 * band_count), jnp.bfloat16),
        pltpu.SemaphoreType.DMA((13,)),
    ]
    for count in (PARTS, max(x_count, 2)):
        scratch += [pltpu.SemaphoreType.DMA((count - 1,))] * 2
    scratch += [pltpu.SemaphoreType.DMA] * 2
    large = pl.BlockSpec(memory_space=pl.ANY)
    visibilities = pl.pallas_call(
        functools.partial(kernel, z_count, x_count, half),
        out_shape=jax.ShapeDtypeStruct((blocks, 2 * LOW), jnp.float32),
        in_specs=[large] * (6 + len(constants)),
        out_specs=pl.BlockSpec(memory_space=pltpu.VMEM),
        scratch_shapes=scratch,
        compiler_params=pltpu.CompilerParams(collective_id=0, has_side_effects=True, vmem_limit_bytes=26 * 2**20),
    )(*[
        pltpu.with_memory_space_constraint(value, pltpu.HBM)
        for value in (sub_owner, sub_offset.T, tile_list, chan_coord, taylor, fourier, *[jnp.asarray(table) for table in constants])
    ])
    return visibilities[:, None, :]


def solution(mesh):
    return jax.shard_map(
        functools.partial(local, mesh.shape["facet"] // PARTS, mesh.shape["chan"]),
        mesh=mesh,
        in_specs=(
            P("facet", "chan", None, None),
            P(),
            P(),
            P(),
            P("facet"),
            P("facet", "chan", None, None),
        ),
        out_specs=P("facet", "chan", None),
        check_vma=False,
    )
```
